32 devices in a mesh: brick: 8 (over z, x), spec: 4 (over y, core).
Axes of the slice: x: 2, y: 2, z: 4, core: 2. Of those that a mesh axis runs over, the one named last changes fastest.
Arguments:
- rhs: float32 [4, 16, 256, 256], P('spec', 'brick'), may hold values from -24 to 24
- density: float32 [16, 256, 256], P('brick', 'spec'), may hold values from 0.01 to 0.1
- kappa: float32 [4], P('spec'), may hold values from 0.5 to 4
- block_group: int32 [8, 16], replicated, may hold values from 0 to 31, as said below
Outputs:
- solution: float32 [4, 16, 256, 256], P('spec', 'brick')
- residual: float32 [4, 16, 256, 256], P('spec', 'brick')
The draws below stay inside these ranges and needn't reach their ends.
Inputs may be any that keep to these rules, and one draw needn't show every extreme that they name: `block_group`: every aggregate id 0 to 31 names at least one block; the blocks of one aggregate share one tile position and lie on consecutive bricks.
All inputs are finite; a program needn't handle non-finite values.
Results may differ from the reference program's by a relative error of at most 0.0003.
Values sent between devices are 32-bit elements; how exact they have to be, the bound alone decides.
A program may use at most 64 MiB of HBM per device.

```python
import math
import jax
import jax.numpy as jnp
from jax import lax

CX = 2
NY = 256
NZ = 256
TILES = 4
CYCLES = 1
COARSE_SWEEPS = 3
SPECIES = 4
NX = 16
NBLK = 16
NAGG = 32
SEGS = 2


def draw_block_group(key, part):
    first_key, second_key = jax.random.split(key)
    bricks = NX // CX
    tile_keys = jax.random.split(first_key, NBLK)
    orders = jax.vmap(lambda single: jax.random.permutation(single, bricks - 1))(tile_keys)
    cuts = (orders < SEGS - 1).astype(jnp.int32)
    segment = jnp.concatenate([jnp.zeros((NBLK, 1), jnp.int32), jnp.cumsum(cuts, axis=1).astype(jnp.int32)], axis=1)
    labels = jnp.arange(NBLK, dtype=jnp.int32)[:, None] * SEGS + segment
    relabel = jax.random.permutation(second_key, NAGG).astype(jnp.int32)
    return jnp.take(relabel, labels.T, axis=0).astype(jnp.int32)


def steps_of(key, shape, shards, least, high):
    factor_of = 1.0
    for position, parts in shards:
        heights = jax.random.uniform(jax.random.fold_in(jax.random.fold_in(key, 6), position), (parts,), jnp.float32, least / len(shards), high / len(shards))
        factor_of = factor_of * jnp.repeat(jnp.exp(heights), shape[position] // parts).reshape((-1,) + (1,) * (len(shape) - 1 - position))
    return factor_of


def gaussian(rng, shape, spread, bound, shards=(), kind=jnp.bfloat16):
    entries = spread * jax.random.normal(rng, shape, jnp.float32)
    if shards:
        entries = entries * steps_of(rng, shape, shards, -0.22, 0.18)
    return jnp.clip(entries, -bound, bound).astype(kind)


def setup_inputs(seed: int = 0) -> dict:
    key_of = jax.random.split(jax.random.key(seed), 5)
    return {
        "rhs": gaussian(key_of[0], (SPECIES, NX, NY, NZ), 4.0, 24.0, ((0, 4), (1, 8)), jnp.float32),
        "density": jnp.clip(jnp.exp(math.log(0.1) - 2.3025851 * jax.random.uniform(key_of[1], (NX, NY, NZ), jnp.float32) ** steps_of(key_of[1], (NX, NY, NZ), ((0, 8), (1, 4)), -0.2, 0.2)), 0.01, 0.1),
        "kappa": jnp.clip(jnp.exp(math.log(4.0) - 2.0794415 * jax.random.uniform(key_of[2], (SPECIES,), jnp.float32) ** steps_of(key_of[2], (SPECIES,), ((0, 4),), -0.2, 0.2)), 0.5, 4.0),
        "block_group": draw_block_group(jax.random.fold_in(key_of[4], 71), 0),
    }


relax_fine = 0.85
relax_coarse = 0.6


def filter_along(field, axis):
    length = field.shape[axis]
    widths = [(0, 0)] * field.ndim
    widths[axis] = (1, 1)
    padded = jnp.pad(field, widths)
    lower = lax.slice_in_dim(padded, 0, length, axis=axis)
    upper = lax.slice_in_dim(padded, 2, length + 2, axis=axis)
    return field + 0.5 * (lower + upper)


def stencil_sum(field):
    return filter_along(filter_along(filter_along(field, 1), 2), 3)


def operate(field, center, scale):
    return center * field - 2.0 * scale * stencil_sum(field)


def relax(field, source, center, diagonal, scale):
    return field + relax_fine * (source - operate(field, center, scale)) / diagonal


def coarsen(field):
    leading = field.shape[:-3]
    first, second, third = field.shape[-3:]
    count = len(leading)
    blocks = field.reshape(leading + (first // 2, 2, second // 2, 2, third // 2, 2))
    return jnp.sum(blocks, axis=(count + 1, count + 3, count + 5)) * 0.125


def refine(field):
    leading = field.shape[:-3]
    first, second, third = field.shape[-3:]
    shaped = field.reshape(leading + (first, 1, second, 1, third, 1))
    grown = jnp.broadcast_to(shaped, leading + (first, 2, second, 2, third, 2))
    return grown.reshape(leading + (2 * first, 2 * second, 2 * third))


def cell_groups(rows, thickness, height, width):
    count = rows.shape[0]
    shaped = rows.reshape(count, 1, TILES, 1, TILES, 1)
    grown = jnp.broadcast_to(shaped, (count, thickness, TILES, height // TILES, TILES, width // TILES))
    return grown.reshape(count * thickness, height, width)


def same_weight(padded, extent):
    first, second, third = extent
    center = padded[1:1 + first, 1:1 + second, 1:1 + third]
    total = jnp.zeros(extent, jnp.float32)
    for first_step in (-1, 0, 1):
        for second_step in (-1, 0, 1):
            for third_step in (-1, 0, 1):
                weight = 0.5 ** (abs(first_step) + abs(second_step) + abs(third_step))
                shifted = lax.slice(padded, (1 + first_step, 1 + second_step, 1 + third_step),
                                    (1 + first_step + first, 1 + second_step + second, 1 + third_step + third))
                total = total + weight * (shifted == center).astype(jnp.float32)
    return total


def group_sums(field, groups):
    flat = groups.reshape(-1)
    return jax.vmap(lambda layer: jax.ops.segment_sum(layer.reshape(-1), flat, num_segments=NAGG))(field)


def reference(rhs, density, kappa, block_group):
    scale = kappa[:, None, None, None]
    center = density[None] + 16.0 * scale
    diagonal = density[None] + 14.0 * scale
    density_coarse = coarsen(density)
    scale_coarse = 0.25 * scale
    center_coarse = density_coarse[None] + 16.0 * scale_coarse
    diagonal_coarse = density_coarse[None] + 14.0 * scale_coarse
    groups = cell_groups(block_group, CX // 2, NY // 2, NZ // 2)
    padded = jnp.pad(groups, 1, constant_values=-1)
    same = same_weight(padded, groups.shape)
    totals = group_sums(jnp.stack([density_coarse, 16.0 - 2.0 * same]), groups)
    coarse_diag = totals[0][None] + (0.25 * kappa)[:, None] * totals[1][None]
    solution = jnp.zeros_like(rhs)
    for cycle in range(CYCLES):
        solution = relax(solution, rhs, center, diagonal, scale)
        solution = relax(solution, rhs, center, diagonal, scale)
        fine_res = rhs - operate(solution, center, scale)
        coarse_res = coarsen(fine_res)
        correction = relax(jnp.zeros_like(coarse_res), coarse_res, center_coarse, diagonal_coarse, scale_coarse)
        correction = relax(correction, coarse_res, center_coarse, diagonal_coarse, scale_coarse)
        remainder = coarse_res - operate(correction, center_coarse, scale_coarse)
        group_rhs = group_sums(remainder, groups)
        group_fix = relax_coarse * group_rhs / coarse_diag
        for sweep in range(COARSE_SWEEPS - 1):
            image = operate(jnp.take(group_fix, groups, axis=1), center_coarse, scale_coarse)
            group_fix = group_fix + relax_coarse * (group_rhs - group_sums(image, groups)) / coarse_diag
        correction = correction + jnp.take(group_fix, groups, axis=1)
        correction = relax(correction, coarse_res, center_coarse, diagonal_coarse, scale_coarse)
        correction = relax(correction, coarse_res, center_coarse, diagonal_coarse, scale_coarse)
        solution = solution + refine(correction)
        solution = relax(solution, rhs, center, diagonal, scale)
        solution = relax(solution, rhs, center, diagonal, scale)
    residual = rhs - operate(solution, center, scale)
    return solution, residual
```

```python
import functools

import jax
import jax.numpy as jnp
from jax import lax
from jax.experimental import pallas as pl
from jax.experimental.pallas import tpu as pltpu
from jax.sharding import PartitionSpec as P

TILES = 4
COARSE_SWEEPS = 3
CHUNKS = 16
AHEAD = 16
relax_fine = 0.85
relax_coarse = 0.6
MESH = pl.DeviceIdType.MESH
F32 = jnp.float32
BF16 = jnp.bfloat16


def iota(shape, dim):
    return lax.broadcasted_iota(jnp.int32, shape, dim)


def split(x, parts):
    out = []
    for _ in range(parts):
        piece = x.astype(BF16)
        out.append(piece)
        x = x - piece.astype(F32)
    return out


def dot(a, b):
    return jnp.dot(a, b, preferred_element_type=F32)


def filter_rows(m):
    size = m.shape[0]
    row = iota(m.shape, 0)
    before = jnp.where(row == 0, 0.0, pltpu.roll(m, 1, 0))
    after = jnp.where(row == size - 1, 0.0, pltpu.roll(m, size - 1, 0))
    return m + 0.5 * (before + after)


def filter_lanes(m):
    size = m.shape[1]
    lane = iota(m.shape, 1)
    before = jnp.where(lane == 0, 0.0, pltpu.roll(m, 1, 1))
    after = jnp.where(lane == size - 1, 0.0, pltpu.roll(m, size - 1, 1))
    return m + 0.5 * (before + after)


def stencil(low, mid, high):
    return filter_lanes(filter_rows(mid + 0.5 * (low + high)))


def pair_matrix(fine, coarse):
    return (iota((coarse, fine), 1) // 2 == iota((coarse, fine), 0)).astype(BF16)


def pair_matrix_t(fine, coarse):
    return (iota((fine, coarse), 0) // 2 == iota((fine, coarse), 1)).astype(BF16)


def coarsen_sum(x):
    rows, cols = x.shape
    left = pair_matrix(rows, rows // 2)
    right = pair_matrix_t(cols, cols // 2)
    halves = sum(dot(left, piece) for piece in split(x, 2))
    return sum(dot(piece, right) for piece in split(halves, 2)) * 0.125


def refine_layer(c):
    rows, cols = c.shape
    left = pair_matrix_t(2 * rows, rows)
    right = pair_matrix(2 * cols, cols)
    total = None
    for piece in split(c, 2):
        term = dot(dot(left, piece).astype(BF16), right)
        total = term if total is None else total + term
    return total


def kernel(
    n, spec, kappa_hbm, bg_hbm, rhs_ref, dens_ref, sol_ref, res_ref,
    kappa_ref, bg_ref,
    R, D, I, V1, V, S, CR, DC, CI, CA, CB, RS, DSUM, FX,
    prs, prr, frs, frr, dss, dsr, gss, gsr,
    azs, aps, ar, ass, asr, bzs, bps, br, vs, vr, ls,
):
    me = lax.axis_index("brick")
    j = lax.axis_index("spec")
    odd = lax.rem(me, 2)
    partner = me + 1 - 2 * odd
    ny, nz = rhs_ref.shape[1], rhs_ref.shape[2]
    hy, hz = ny // 2, nz // 2
    rows = dens_ref.shape[1]
    half = n // 2
    pslot = 2 - 2 * odd
    fslot = 2 * odd
    fdest = me + 2 - 4 * odd
    fsends = jnp.logical_and(fdest >= 0, fdest < n)
    fsource = me - 2 + 4 * odd
    frecvs = jnp.logical_and(fsource >= 0, fsource < n)
    fdest_c = lax.rem(fdest + n, n)
    fsource_c = lax.rem(fsource + n, n)
    core = j + 1 - 2 * lax.rem(j, 2)
    far = lax.rem(j + spec // 2, spec)
    chunk = ny // CHUNKS

    def remote(src, dst, ssem, rsem, b, s):
        return pltpu.make_async_remote_copy(
            src_ref=src, dst_ref=dst, send_sem=ssem, recv_sem=rsem,
            device_id={"brick": b, "spec": s}, device_id_type=MESH,
        )

    barrier = pltpu.get_barrier_semaphore()
    for k in range(1, half):
        pl.semaphore_signal(barrier, inc=1, device_id={"brick": lax.rem(me + 2 * k, n), "spec": j}, device_id_type=MESH)
    pl.semaphore_signal(barrier, inc=1, device_id={"brick": partner, "spec": j}, device_id_type=MESH)
    pl.semaphore_signal(barrier, inc=1, device_id={"brick": me, "spec": core}, device_id_type=MESH)
    pl.semaphore_signal(barrier, inc=1, device_id={"brick": me, "spec": far}, device_id_type=MESH)

    my_rows = pl.ds(pl.multiple_of(j * rows, 8), rows)
    core_rows = pl.ds(pl.multiple_of(core * rows, 8), rows)
    far_rows = pl.ds(pl.multiple_of(far * rows, 8), rows)
    far_core = lax.rem(core + spec // 2, spec)
    far_core_rows = pl.ds(pl.multiple_of(far_core * rows, 8), rows)
    loads = [
        pltpu.make_async_copy(dens_ref, D.at[1, :, my_rows, :], ls.at[0]),
        pltpu.make_async_copy(kappa_hbm, kappa_ref, ls.at[1]),
        pltpu.make_async_copy(bg_hbm, bg_ref, ls.at[2]),
        pltpu.make_async_copy(rhs_ref, R.at[1], ls.at[3]),
    ]
    for load in loads:
        load.start()
    crows = rows // 2
    cmine = pl.ds(pl.multiple_of(j * crows, 8), crows)
    ccore = pl.ds(pl.multiple_of(core * crows, 8), crows)
    cfar = pl.ds(pl.multiple_of(far * crows, 8), crows)
    cfarcore = pl.ds(pl.multiple_of(far_core * crows, 8), crows)

    V1[0] = jnp.zeros((ny, nz), F32)
    V1[7] = jnp.zeros((ny, nz), F32)
    zero = jnp.zeros((hy, hz), F32)
    for buf in (CA, CB):
        buf[0] = zero
        buf[n + 1] = zero
    for load in loads:
        load.wait()
    kap = kappa_ref[0]
    kap1 = 0.25 * kap
    DC[me, cmine, :] = coarsen_sum(D[1, 0, my_rows, :] + D[1, 1, my_rows, :])
    pl.semaphore_wait(barrier, half - 1 + 3)

    dslot = 2 * odd
    dpair = remote(dens_ref, D.at[dslot, :, my_rows, :], dss.at[0], dsr.at[0], partner, j)
    dpair.start()
    dpair_in = remote(dens_ref, D.at[pslot, :, my_rows, :], dss.at[0], dsr.at[0], partner, j)

    def rchunk(c):
        return pl.ds(pl.multiple_of(c * chunk, 8), chunk)

    def rpair(c, slot):
        return remote(rhs_ref.at[:, rchunk(c), :], R.at[slot, :, rchunk(c), :], prs.at[c], prr.at[c], partner, j)

    def rfwd(c, slot, dest):
        return remote(R.at[pslot, :, rchunk(c), :], R.at[slot, :, rchunk(c), :], frs.at[c], frr.at[c], dest, j)

    slots = (1, pslot, fslot)

    def dsrc(kind):
        return dens_ref if kind == 0 else D.at[slots[kind], :, my_rows, :]

    def dfar(kind, at):
        return remote(dsrc(kind), D.at[slots[kind], :, at, :], gss.at[kind, 0], gsr.at[kind, 0], me, far)

    def dcore(kind, at):
        return remote(dsrc(kind), D.at[slots[kind], :, at, :], gss.at[kind, 1], gsr.at[kind, 1], me, core)

    def dcorefar(kind, at):
        return remote(D.at[slots[kind], :, far_rows, :], D.at[slots[kind], :, at, :], gss.at[kind, 2], gsr.at[kind, 2], me, core)

    dfar(0, my_rows).start()
    dcore(0, my_rows).start()

    def gather_start(view, zs, ps, rs):
        for k in range(1, half):
            remote(view(me), view(me), zs.at[k], rs.at[me], lax.rem(me + 2 * k, n), j).start()
        remote(view(me), view(me), ps.at[0], rs.at[me], partner, j).start()

    def gather_forward(view, zs, ps, rs):
        for k in range(1, half):
            b = lax.rem(me + 2 * k, n)
            remote(view(b), view(b), zs.at[k], rs.at[b], partner, j).wait_recv()
            remote(view(b), view(b), ps.at[k], rs.at[b], partner, j).start()

    def gather_finish(view, zs, ps, rs):
        for k in range(half):
            b = lax.rem(partner + 2 * k, n)
            remote(view(b), view(b), ps.at[k], rs.at[b], partner, j).wait_recv()

    def gather_sent(view, zs, ps, rs):
        for k in range(1, half):
            remote(view(me), view(me), zs.at[k], rs.at[me], partner, j).wait_send()
        for k in range(half):
            remote(view(me), view(me), ps.at[k], rs.at[me], partner, j).wait_send()

    dview = lambda b: DC.at[b, cmine, :]
    dgather = (dview, azs, aps, ar)
    gather_start(*dgather)
    for c in range(AHEAD):
        rpair(c, dslot).start()

    def cfar_copy(at):
        return remote(DC.at[:, cmine, :], DC.at[:, at, :], ass.at[0], asr.at[0], me, far)

    def ccore_copy(at):
        return remote(DC.at[:, cmine, :], DC.at[:, at, :], ass.at[1], asr.at[1], me, core)

    def ccorefar_copy(at):
        return remote(DC.at[:, cfar, :], DC.at[:, at, :], ass.at[2], asr.at[2], me, core)

    dpair_in.wait_recv()

    def dfwd(slot, dest):
        return remote(D.at[pslot, :, my_rows, :], D.at[slot, :, my_rows, :], dss.at[1], dsr.at[1], dest, j)

    @pl.when(fsends)
    def _():
        dfwd(2 * odd, fdest_c).start()

    dfar(1, my_rows).start()
    dcore(1, my_rows).start()

    def gather_forward_one(view, zs, ps, rs, k):
        b = lax.rem(me + 2 * k, n)
        remote(view(b), view(b), zs.at[k], rs.at[b], partner, j).wait_recv()
        remote(view(b), view(b), ps.at[k], rs.at[b], partner, j).start()

    for c in range(CHUNKS):
        rpair(c, pslot).wait_recv()
        if c + AHEAD < CHUNKS:
            rpair(c + AHEAD, dslot).start()

        @pl.when(fsends)
        def _():
            rfwd(c, 2 * odd, fdest_c).start()

        if c == 1:
            dfar(0, far_rows).wait_recv()
            dcorefar(0, far_rows).start()
            gather_forward(*dgather)
        if c == 1:
            dfar(1, far_rows).wait_recv()
            dcorefar(1, far_rows).start()

            @pl.when(frecvs)
            def _():
                dfwd(fslot, fsource_c).wait_recv()
                dfar(2, my_rows).start()
                dcore(2, my_rows).start()

        if c == CHUNKS - 1:
            gather_finish(*dgather)
            cfar_copy(cmine).start()
            ccore_copy(cmine).start()
        if c == 11:
            @pl.when(frecvs)
            def _():
                dfar(2, far_rows).wait_recv()
                dcorefar(2, far_rows).start()


    def prepare(slot, valid):
        def body(i, carry):
            inv = relax_fine / (D[slot, i] + 14.0 * kap)
            I[slot, i] = inv
            first = R[slot, i] * inv
            V1[2 * slot + i + 1] = first if valid is None else jnp.where(valid, first, 0.0)
            return carry

        lax.fori_loop(0, 2, body, 0)

    dcore(0, core_rows).wait_recv()
    dcorefar(0, far_core_rows).wait_recv()
    prepare(1, None)
    dcore(1, core_rows).wait_recv()
    dcorefar(1, far_core_rows).wait_recv()
    prepare(pslot, None)

    def inside(e):
        g = 2 * me + e - 3
        return jnp.logical_and(g >= 0, g < 2 * n)

    def relax_layer(src, e):
        slot, i = (e - 1) // 2, lax.rem(e - 1, 2)
        v = src[e]
        f = stencil(src[e - 1], v, src[e + 1])
        out = (1.0 - relax_fine) * v + I[slot, i] * (R[slot, i] + 2.0 * kap * (f - v))
        return jnp.where(inside(e), out, 0.0)

    def residual_layer(src, e):
        i = e - 3
        v = src[e]
        f = stencil(src[e - 1], v, src[e + 1])
        return R[1, i] - (D[1, i] + 16.0 * kap) * v + 2.0 * kap * f

    base = 4 - 2 * odd
    other = 2 + 2 * odd

    def vout(i):
        return remote(V.at[base + i], V.at[6 * odd + i], vs.at[0, i], vr.at[0, i], fdest_c, j)

    def vback(i):
        return remote(V.at[other + i], V.at[6 - 6 * odd + i], vs.at[1, i], vr.at[1, i], fsource_c, j)

    def vout_in(i):
        return remote(V.at[base + i], V.at[6 * odd + i], vs.at[0, i], vr.at[0, i], fsource_c, j)

    def vback_in(i):
        return remote(V.at[other + i], V.at[6 - 6 * odd + i], vs.at[1, i], vr.at[1, i], fdest_c, j)

    def second(e):
        V[e] = relax_layer(V1, e)

    second(base)

    second(base + 1)

    @pl.when(frecvs)
    def _():
        dcore(2, core_rows).wait_recv()
        dcorefar(2, far_core_rows).wait_recv()
        for c in range(CHUNKS):
            rfwd(c, fslot, fsource_c).wait_recv()
        prepare(fslot, None)

    @pl.when(jnp.logical_not(frecvs))
    def _():
        for i in range(2):
            V1[2 * fslot + i + 1] = jnp.zeros((ny, nz), F32)

    second(other)
    second(other + 1)
    CR[me] = coarsen_sum(residual_layer(V, 3) + residual_layer(V, 4))
    rview = lambda b: CR.at[b]
    rgather = (rview, bzs, bps, br)
    gather_start(*rgather)

    @pl.when(fsends)
    def _():
        vout(0).start()
        vout(1).start()

    @pl.when(frecvs)
    def _():
        vback(0).start()
        vback(1).start()

    cfar_copy(cfar).wait_recv()
    ccorefar_copy(cfar).start()
    gather_forward(*rgather)
    ccore_copy(ccore).wait_recv()
    ccorefar_copy(cfarcore).wait_recv()

    edge = hy // TILES
    lane_tile = iota((hz, hz), 0) // (hz // TILES) == iota((hz, hz), 1) // (hz // TILES)
    same_tile = lane_tile.astype(BF16)

    def lane_sums(x):
        return sum(dot(piece, same_tile) for piece in split(x, 3))

    bgf = bg_ref[...].astype(F32).astype(BF16)
    ids = []
    for ty in range(TILES):
        pick = iota((TILES * TILES, hz), 0) == ty * TILES + iota((TILES * TILES, hz), 1) // (hz // TILES)
        ids.append(dot(bgf, pick.astype(BF16)))

    brick_row = iota((n, hz), 0)
    lane = iota((n, hz), 1)
    tile_lanes = hz // TILES

    def lower_brick(x, fill):
        return jnp.where(brick_row == 0, fill, pltpu.roll(x, 1, 0))

    def upper_brick(x, fill):
        return jnp.where(brick_row == n - 1, fill, pltpu.roll(x, n - 1, 0))

    def group_sums(fields):
        out = []
        for ty in range(TILES):
            total = jnp.zeros((n, hz), F32)
            for b in range(n):
                total = total + jnp.where(ids[ty][b : b + 1] == ids[ty], fields[ty][b : b + 1], 0.0)
            out.append(total)
        return out

    def coarse_first(b, carry):
        d = DC[b]
        CI[b] = relax_fine / (d + 14.0 * kap1)
        for ty in range(TILES):
            DSUM[ty, pl.ds(b, 1), :] = jnp.sum(d[ty * edge : (ty + 1) * edge], axis=0, keepdims=True)
        return carry

    lax.fori_loop(0, n, coarse_first, 0)
    dens_sum = [lane_sums(DSUM[ty]) for ty in range(TILES)]
    weight = []
    for ty in range(TILES):
        fx = 1.0 + 0.5 * (lower_brick(ids[ty], -1.0) == ids[ty]).astype(F32)
        fx = fx + 0.5 * (upper_brick(ids[ty], -1.0) == ids[ty]).astype(F32)
        cells = edge * tile_lanes
        weight.append(16.0 * cells - 2.0 * (2 * edge - 1) * (2 * tile_lanes - 1) * fx)
    totals0 = group_sums(dens_sum)
    totals1 = group_sums(weight)
    step = [relax_coarse / (totals0[ty] + kap1 * totals1[ty]) for ty in range(TILES)]

    @pl.when(me == 1)
    def _():
        V[1] = relax_layer(V1, 1)
        V[0] = jnp.zeros((ny, nz), F32)

    @pl.when(me == 0)
    def _():
        V[0] = jnp.zeros((ny, nz), F32)
        V[1] = jnp.zeros((ny, nz), F32)

    @pl.when(me == n - 2)
    def _():
        V[6] = relax_layer(V1, 6)
        V[7] = jnp.zeros((ny, nz), F32)

    @pl.when(me == n - 1)
    def _():
        V[6] = jnp.zeros((ny, nz), F32)
        V[7] = jnp.zeros((ny, nz), F32)

    gather_finish(*rgather)

    def coarse_start(b, carry):
        CA[b + 1] = CR[b] * CI[b]
        return carry

    lax.fori_loop(0, n, coarse_start, 0)

    def coarse_defect(src, b):
        v = src[b + 1]
        f = stencil(src[b], v, src[b + 2])
        return v, CR[b] - (DC[b] + 16.0 * kap1) * v + 2.0 * kap1 * f

    def coarse_relax(src, dst):
        def body(b, carry):
            v = src[b + 1]
            f = stencil(src[b], v, src[b + 2])
            dst[b + 1] = (1.0 - relax_fine) * v + CI[b] * (CR[b] + 2.0 * kap1 * (f - v))
            return carry

        return body

    lax.fori_loop(0, n, coarse_relax(CA, CB), 0)

    def remainder(b, carry):
        defect = coarse_defect(CB, b)[1]
        for ty in range(TILES):
            RS[ty, pl.ds(b, 1), :] = jnp.sum(defect[ty * edge : (ty + 1) * edge], axis=0, keepdims=True)
        return carry

    lax.fori_loop(0, n, remainder, 0)
    group_rhs = group_sums([lane_sums(RS[ty]) for ty in range(TILES)])
    fix = [step[ty] * group_rhs[ty] for ty in range(TILES)]

    def aggregate_image(g):
        along = [x + 0.5 * (lower_brick(x, 0.0) + upper_brick(x, 0.0)) for x in g]
        blank = jnp.zeros((n, hz), F32)
        out = []
        for ty in range(TILES):
            below = along[ty - 1] if ty > 0 else blank
            above = along[ty + 1] if ty < TILES - 1 else blank
            mid = (2.0 * edge - 1.0) * along[ty] + 0.5 * (below + above)
            left = jnp.where(lane < tile_lanes, 0.0, pltpu.roll(mid, tile_lanes, 1))
            right = jnp.where(lane >= hz - tile_lanes, 0.0, pltpu.roll(mid, hz - tile_lanes, 1))
            f = (2.0 * tile_lanes - 1.0) * mid + 0.5 * (left + right)
            own = dens_sum[ty] + 16.0 * kap1 * (edge * tile_lanes)
            out.append(own * g[ty] - 2.0 * kap1 * f)
        return group_sums(out)

    for _ in range(COARSE_SWEEPS - 1):
        image = aggregate_image(fix)
        fix = [fix[ty] + step[ty] * (group_rhs[ty] - image[ty]) for ty in range(TILES)]
    for ty in range(TILES):
        FX[ty] = fix[ty]

    def add_fix(b, carry):
        for ty in range(TILES):
            part = pl.ds(ty * edge, edge)
            CA[b + 1, part, :] = CB[b + 1, part, :] + FX[ty, pl.ds(b, 1), :]
        return carry

    def near(width):
        return jnp.maximum(me - width, 0), jnp.minimum(me + width + 1, n)

    lax.fori_loop(*near(4), add_fix, 0)
    lax.fori_loop(*near(3), coarse_relax(CA, CB), 0)
    lax.fori_loop(*near(2), coarse_relax(CB, CA), 0)

    def inner(t, carry):
        b = me + t - 2
        valid = jnp.logical_and(b >= 0, b < n)
        fine = refine_layer(CA[jnp.clip(b, 0, n - 1) + 1])
        for e, add in ((2 * t - 1, t > 1), (2 * t, t < 3)):
            S[e] = jnp.where(valid, V[e] + fine if add else fine, 0.0)
        return carry

    for t in (1, 2, 3):
        inner(t, 0)
    for t, e in ((0, 0), (4, 7)):
        b = me + t - 2
        valid = jnp.logical_and(b >= 0, b < n)
        S[e] = jnp.where(valid, refine_layer(CA[jnp.clip(b, 0, n - 1) + 1]), 0.0)

    def third(e, carry):
        V1[e] = relax_layer(S, e)
        return carry

    lax.fori_loop(3, 5, third, 0)

    @pl.when(frecvs)
    def _():
        vout_in(0).wait_recv()
        vout_in(1).wait_recv()

    @pl.when(fsends)
    def _():
        vback_in(0).wait_recv()
        vback_in(1).wait_recv()

    for e in (0, 1, 6, 7):
        S[e] = jnp.where(inside(e), S[e] + V[e], 0.0)
    lax.fori_loop(1, 3, third, 0)
    lax.fori_loop(5, 7, third, 0)

    def fourth(e, carry):
        S[e] = relax_layer(V1, e)
        return carry

    lax.fori_loop(2, 6, fourth, 0)

    def last(i, carry):
        sol_ref[i] = S[i + 3]
        res_ref[i] = residual_layer(S, i + 3)
        return carry

    lax.fori_loop(0, 2, last, 0)

    dpair.wait_send()
    for c in range(CHUNKS):
        rpair(c, dslot).wait_send()
    for kind in (0, 1):
        dfar(kind, my_rows).wait_send()
        dcore(kind, my_rows).wait_send()
        dcorefar(kind, far_rows).wait_send()

    @pl.when(frecvs)
    def _():
        dfar(2, my_rows).wait_send()
        dcore(2, my_rows).wait_send()
        dcorefar(2, far_rows).wait_send()

    @pl.when(fsends)
    def _():
        dfwd(2 * odd, fdest_c).wait_send()
        for c in range(CHUNKS):
            rfwd(c, 2 * odd, fdest_c).wait_send()

    gather_sent(*dgather)
    gather_sent(*rgather)
    cfar_copy(cmine).wait_send()
    ccore_copy(cmine).wait_send()
    ccorefar_copy(cfar).wait_send()

    @pl.when(fsends)
    def _():
        vout(0).wait_send()
        vout(1).wait_send()

    @pl.when(frecvs)
    def _():
        vback(0).wait_send()
        vback(1).wait_send()


def local(n, spec, rhs, density, kappa, block_group):
    _, cells, ny, nz = rhs.shape
    hy, hz = ny // 2, nz // 2
    fine = lambda *lead: pltpu.VMEM(lead + (ny, nz), F32)
    coarse = lambda *lead: pltpu.VMEM(lead + (hy, hz), F32)
    dma = lambda *shape: pltpu.SemaphoreType.DMA(shape)
    vmem = pl.BlockSpec(memory_space=pltpu.VMEM)
    out = jax.ShapeDtypeStruct((cells, ny, nz), F32)
    hbm = lambda x: pltpu.with_memory_space_constraint(x, pltpu.HBM)
    sol, res = pl.pallas_call(
        functools.partial(kernel, n, spec),
        out_shape=(out, out),
        in_specs=[pl.BlockSpec(memory_space=pltpu.HBM)] * 4,
        out_specs=(vmem, vmem),
        scratch_shapes=[
            pltpu.SMEM((1,), F32), pltpu.VMEM(block_group.shape, jnp.int32),
            fine(3, 2), fine(3, 2), fine(3, 2), fine(8), fine(8), fine(8),
            coarse(n), coarse(n), coarse(n), coarse(n + 2), coarse(n + 2),
            pltpu.VMEM((TILES, n, hz), F32), pltpu.VMEM((TILES, n, hz), F32), pltpu.VMEM((TILES, n, hz), F32),
            dma(CHUNKS), dma(CHUNKS), dma(CHUNKS), dma(CHUNKS), dma(2), dma(2), dma(3, 3), dma(3, 3),
            dma(n // 2), dma(n // 2), dma(n), dma(3), dma(3),
            dma(n // 2), dma(n // 2), dma(n), dma(2, 2), dma(2, 2), dma(4),
        ],
        compiler_params=pltpu.CompilerParams(
            collective_id=0, has_side_effects=True, vmem_limit_bytes=(20 << 20) + 24 * n * hy * hz
        ),
    )(kappa, hbm(block_group), hbm(rhs.reshape(cells, ny, nz)), hbm(density))
    return sol[None], res[None]


def solution(mesh):
    return jax.shard_map(
        functools.partial(local, mesh.shape["brick"], mesh.shape["spec"]),
        mesh=mesh,
        in_specs=(P("spec", "brick", None, None), P("brick", "spec", None), P("spec"), P()),
        out_specs=(P("spec", "brick", None, None), P("spec", "brick", None, None)),
        check_vma=False,
    )
```

```python
import functools

import jax
import jax.numpy as jnp
from jax import lax
from jax.experimental import pallas as pl
from jax.experimental.pallas import tpu as pltpu
from jax.sharding import PartitionSpec as P

TILES = 4
COARSE_SWEEPS = 3
relax_fine = 0.85
relax_coarse = 0.6
MESH = pl.DeviceIdType.MESH
F32 = jnp.float32
BF16 = jnp.bfloat16


def iota(shape, dim):
    return lax.broadcasted_iota(jnp.int32, shape, dim)


def split(x, parts):
    out = []
    for _ in range(parts):
        piece = x.astype(BF16)
        out.append(piece)
        x = x - piece.astype(F32)
    return out


def dot(a, b):
    return jnp.dot(a, b, preferred_element_type=F32)


def filter_rows(m):
    size = m.shape[0]
    row = iota(m.shape, 0)
    before = jnp.where(row == 0, 0.0, pltpu.roll(m, 1, 0))
    after = jnp.where(row == size - 1, 0.0, pltpu.roll(m, size - 1, 0))
    return m + 0.5 * (before + after)


def filter_lanes(m):
    size = m.shape[1]
    lane = iota(m.shape, 1)
    before = jnp.where(lane == 0, 0.0, pltpu.roll(m, 1, 1))
    after = jnp.where(lane == size - 1, 0.0, pltpu.roll(m, size - 1, 1))
    return m + 0.5 * (before + after)


def stencil(low, mid, high):
    return filter_lanes(filter_rows(mid + 0.5 * (low + high)))


def pair_matrix(fine, coarse):
    return (iota((coarse, fine), 1) // 2 == iota((coarse, fine), 0)).astype(BF16)


def pair_matrix_t(fine, coarse):
    return (iota((fine, coarse), 0) // 2 == iota((fine, coarse), 1)).astype(BF16)


def coarsen_sum(x, left=None):
    rows, cols = x.shape
    if left is None:
        left = pair_matrix(rows, rows // 2)
    right = pair_matrix_t(cols, cols // 2)
    halves = sum(dot(left, piece) for piece in split(x, 2))
    return sum(dot(piece, right) for piece in split(halves, 2)) * 0.125


def pieces_of(rows):
    units = rows // 8
    sizes = [max(1, round(units * share)) for share in (0.3, 0.3, 0.22, 0.12)]
    sizes.append(units - sum(sizes))
    starts = [sum(sizes[:c]) for c in range(len(sizes))]
    return [(8 * start, 8 * size) for start, size in zip(starts, sizes)]


def refine_layer(c):
    rows, cols = c.shape
    left = pair_matrix_t(2 * rows, rows)
    right = pair_matrix(2 * cols, cols)
    total = None
    for piece in split(c, 2):
        term = dot(dot(left, piece).astype(BF16), right)
        total = term if total is None else total + term
    return total


def kernel(
    n, spec, kappa_hbm, bg_hbm, rhs_ref, dens_ref, sol_ref, res_ref,
    kappa_ref, bg_ref,
    R, RF, D, IW, IE, V1, V2, W3, W4, WX, S, E3, CR, DC, CI, CA, CB, RS, DSUM, FX,
    prs, prr, frs, frr, rgs, rgr, dss, dsr, gss, gsr, dgs, dgr,
    azs, aps, ar, ass, asr, bzs, bps, br, w3s, w3r, w4s, w4r, xs, xr, ls,
):
    me = lax.axis_index("brick")
    j = lax.axis_index("spec")
    odd = lax.rem(me, 2)
    even = 1 - odd
    base = me - odd
    partner = base + even
    ny, nz = rhs_ref.shape[1], rhs_ref.shape[2]
    hy, hz = ny // 2, nz // 2
    rows = dens_ref.shape[1]
    half = n // 2
    window = R.shape[1]
    pieces = pieces_of(window)
    down, up = base > 0, base + 2 < n
    flow = jnp.logical_or(jnp.logical_and(odd == 0, down), jnp.logical_and(odd == 1, up))
    fhigh = jnp.logical_or(jnp.logical_and(odd == 0, up), jnp.logical_and(odd == 1, down))
    onward = lax.rem(me + 2 - 4 * odd + n, n)
    back = lax.rem(me - 2 + 4 * odd + n, n)
    below = lax.rem(me - 2 + n, n)
    above = lax.rem(me + 2, n)
    core = j + 1 - 2 * lax.rem(j, 2)
    far = lax.rem(j + spec // 2, spec)
    mine, theirs, near_slot, far_slot = 1 + odd, 2 - odd, 3 * odd, 3 - 3 * odd

    def remote(src, dst, ssem, rsem, b, s):
        return pltpu.make_async_remote_copy(
            src_ref=src, dst_ref=dst, send_sem=ssem, recv_sem=rsem,
            device_id={"brick": b, "spec": s}, device_id_type=MESH,
        )

    barrier = pltpu.get_barrier_semaphore()
    for k in range(1, half):
        pl.semaphore_signal(barrier, inc=1, device_id={"brick": lax.rem(me + 2 * k, n), "spec": j}, device_id_type=MESH)
    pl.semaphore_signal(barrier, inc=1, device_id={"brick": partner, "spec": j}, device_id_type=MESH)
    pl.semaphore_signal(barrier, inc=1, device_id={"brick": me, "spec": core}, device_id_type=MESH)
    pl.semaphore_signal(barrier, inc=1, device_id={"brick": me, "spec": far}, device_id_type=MESH)

    def eight(start, size):
        return pl.ds(pl.multiple_of(start, 8), size)

    far_core = lax.rem(core + spec // 2, spec)
    my_rows, core_rows, far_rows, far_core_rows = [eight(at * rows, rows) for at in (j, core, far, far_core)]
    crows = rows // 2
    cmine, ccore, cfar, cfarcore = [eight(at * crows, crows) for at in (j, core, far, far_core)]
    win = odd * (ny - window)
    their_win = even * (ny - window)
    lead = 8 * odd
    my_half, their_half = eight(odd * hy, hy), eight(even * hy, hy)
    loads = [
        pltpu.make_async_copy(dens_ref, D.at[mine, :, my_rows, :], ls.at[0]),
        pltpu.make_async_copy(kappa_hbm, kappa_ref, ls.at[1]),
        pltpu.make_async_copy(bg_hbm, bg_ref, ls.at[2]),
        pltpu.make_async_copy(rhs_ref.at[:, eight(win, window), :], R.at[pl.ds(2 * mine, 2)], ls.at[3]),
        pltpu.make_async_copy(rhs_ref, RF, ls.at[4]),
    ]
    for load in loads:
        load.start()

    blank = jnp.zeros((window, nz), F32)

    @pl.when(jnp.logical_not(down))
    def _():
        for buf, q in ((V1, 0), (V1, 1), (V2, 1), (W3, 1), (W4, 1)):
            buf[q] = blank

    @pl.when(jnp.logical_not(up))
    def _():
        for buf, q in ((V1, 6), (V1, 7), (V2, 6), (W3, 6), (W4, 6)):
            buf[q] = blank

    zero = jnp.zeros((hy, hz), F32)
    for buf in (CA, CB):
        buf[0] = zero
        buf[n + 1] = zero
    for load in loads[:3]:
        load.wait()
    kap = kappa_ref[0]
    kap1 = 0.25 * kap
    DC[me, cmine, :] = coarsen_sum(D[mine, 0, my_rows, :] + D[mine, 1, my_rows, :])
    pl.semaphore_wait(barrier, half - 1 + 3)

    def dpair(i, slot):
        return remote(dens_ref.at[i], D.at[slot, i, my_rows, :], dss.at[0, i], dsr.at[0, i], partner, j)

    def dfwd(i, dest):
        return remote(D.at[theirs, i, my_rows, :], D.at[near_slot, i, my_rows, :], dss.at[1, i], dsr.at[1, i], dest, j)

    def rpair(c, slot):
        start, size = pieces[c]
        return remote(
            rhs_ref.at[:, eight(their_win + start, size), :], R.at[pl.ds(2 * slot, 2), pl.ds(start, size), :],
            prs.at[c], prr.at[c], partner, j,
        )

    def rfwd(c, dest):
        start, size = pieces[c]
        return remote(
            R.at[pl.ds(2 * theirs, 2), pl.ds(start, size), :], R.at[pl.ds(2 * near_slot, 2), pl.ds(start, size), :],
            frs.at[c], frr.at[c], dest, j,
        )

    def rback(dest):
        return remote(rhs_ref.at[:, eight(win, window), :], R.at[pl.ds(2 * far_slot, 2)], rgs.at[0], rgr.at[0], dest, j)

    slots = (mine, theirs, near_slot)

    def dsrc(kind, i):
        return dens_ref.at[i] if kind == 0 else D.at[slots[kind], i, my_rows, :]

    def dfar(kind, i, at):
        return remote(dsrc(kind, i), D.at[slots[kind], i, at, :], gss.at[kind, 0, i], gsr.at[kind, 0, i], me, far)

    def dcore(kind, i, at):
        return remote(dsrc(kind, i), D.at[slots[kind], i, at, :], gss.at[kind, 1, i], gsr.at[kind, 1, i], me, core)

    def dcorefar(kind, i, at):
        return remote(
            D.at[slots[kind], i, far_rows, :], D.at[slots[kind], i, at, :], gss.at[kind, 2, i], gsr.at[kind, 2, i], me, core
        )

    strip = (hy + 16) // 2
    strip_win = odd * (hy - 16)

    def strip_rows(which):
        return eight(strip_win + strip * which, strip)

    lane_of = lax.rem(j, 2)

    def dback(dest):
        at = strip_rows(lane_of)
        return remote(D.at[mine, :, at, :], D.at[far_slot, :, at, :], dgs.at[0], dgr.at[0], dest, j)

    def dbackcore(which):
        at = strip_rows(which)
        return remote(D.at[far_slot, :, at, :], D.at[far_slot, :, at, :], dgs.at[1], dgr.at[1], me, core)

    def gather_start(view, zs, ps, rs):
        for k in range(1, half):
            remote(view(me), view(me), zs.at[k], rs.at[me], lax.rem(me + 2 * k, n), j).start()
        remote(view(me), view(me), ps.at[0], rs.at[me], partner, j).start()

    def gather_forward(view, zs, ps, rs):
        for k in range(1, half):
            b = lax.rem(me + 2 * k, n)
            remote(view(b), view(b), zs.at[k], rs.at[b], partner, j).wait_recv()
            remote(view(b), view(b), ps.at[k], rs.at[b], partner, j).start()

    def gather_finish(view, zs, ps, rs):
        for k in range(half):
            b = lax.rem(partner + 2 * k, n)
            remote(view(b), view(b), ps.at[k], rs.at[b], partner, j).wait_recv()

    def gather_sent(view, zs, ps, rs):
        for k in range(1, half):
            remote(view(me), view(me), zs.at[k], rs.at[me], partner, j).wait_send()
        for k in range(half):
            remote(view(me), view(me), ps.at[k], rs.at[me], partner, j).wait_send()

    dview = lambda b: DC.at[b, cmine, :]
    dgather = (dview, azs, aps, ar)
    for i in range(2):
        dpair(i, mine).start()
    for i in range(2):
        dfar(0, i, my_rows).start()
        dcore(0, i, my_rows).start()

    @pl.when(flow)
    def _():
        rback(back).start()

    gather_start(*dgather)
    for c in range(len(pieces)):
        rpair(c, mine).start()

    def cfar_copy(at):
        return remote(DC.at[:, cmine, :], DC.at[:, at, :], ass.at[0], asr.at[0], me, far)

    def ccore_copy(at):
        return remote(DC.at[:, cmine, :], DC.at[:, at, :], ass.at[1], asr.at[1], me, core)

    def ccorefar_copy(at):
        return remote(DC.at[:, cfar, :], DC.at[:, at, :], ass.at[2], asr.at[2], me, core)

    for i in range(2):
        dpair(i, theirs).wait_recv()

        @pl.when(fhigh)
        def _():
            dfwd(i, onward).start()

        dfar(1, i, my_rows).start()
        dcore(1, i, my_rows).start()
        dfar(0, i, far_rows).wait_recv()
        dcorefar(0, i, far_rows).start()

    def pass_on(c):
        rpair(c, theirs).wait_recv()

        @pl.when(fhigh)
        def _():
            rfwd(c, onward).start()

    for i in range(2):
        dcore(0, i, core_rows).wait_recv()
        dcorefar(0, i, far_core_rows).wait_recv()

    @pl.when(flow)
    def _():
        dback(back).start()

    pass_on(0)
    pass_on(1)
    gather_forward(*dgather)

    @pl.when(flow)
    def _():
        for i in range(2):
            dfwd(i, back).wait_recv()
            dfar(2, i, my_rows).start()
            dcore(2, i, my_rows).start()

    pass_on(2)
    for i in range(2):
        dfar(1, i, far_rows).wait_recv()
        dcorefar(1, i, far_rows).start()
    for c in range(3, len(pieces)):
        pass_on(c)
    gather_finish(*dgather)
    @pl.when(fhigh)
    def _():
        dback(onward).wait_recv()
        dbackcore(lane_of).start()

    def prepare(slot):
        def body(i, carry):
            inv = relax_fine / (D[slot, i, eight(win, window), :] + 14.0 * kap)
            IW[2 * slot + i] = inv
            V1[2 * slot + i] = R[2 * slot + i] * inv
            return carry

        lax.fori_loop(0, 2, body, 0)

    def layer(k):
        return k + odd * (7 - 2 * k)

    def relax_window(src, dst, q):
        v = src[q]
        f = stencil(src[q - 1], v, src[q + 1])
        dst[q] = (1.0 - relax_fine) * v + IW[q] * (R[q] + 2.0 * kap * (f - v))

    def residual_window(q):
        v = V2[q]
        f = stencil(V2[q - 1], v, V2[q + 1])
        d = D[q // 2, lax.rem(q, 2), eight(win, window), :]
        return R[q] - (d + 16.0 * kap) * v + 2.0 * kap * f

    chalf = hy // 2
    pick = (iota((chalf, window), 1) // 2 - lead // 2 == iota((chalf, window), 0)).astype(BF16)

    def coarse_rows_of(parity):
        return eight(parity * chalf, chalf)

    def restrict(q, brick):
        CR[brick, coarse_rows_of(odd), :] = coarsen_sum(residual_window(q) + residual_window(q + 1), pick)

    loads[3].wait()
    loads[4].wait()
    prepare(mine)

    @pl.when(flow)
    def _():
        for i in range(2):
            dfar(2, i, far_rows).wait_recv()
            dcorefar(2, i, far_rows).start()

    cfar_copy(cmine).start()
    ccore_copy(cmine).start()
    for i in range(2):
        dcore(1, i, core_rows).wait_recv()
        dcorefar(1, i, far_core_rows).wait_recv()
    prepare(theirs)
    for k in (3, 4):
        relax_window(V1, V2, layer(k))

    @pl.when(fhigh)
    def _():
        rback(onward).wait_recv()
        dbackcore(1 - lane_of).wait_recv()
        prepare(far_slot)

    relax_window(V1, V2, layer(5))

    @pl.when(fhigh)
    def _():
        relax_window(V1, V2, layer(6))

    restrict(4 - 2 * odd, base + even)

    @pl.when(flow)
    def _():
        for i in range(2):
            dcore(2, i, core_rows).wait_recv()
            dcorefar(2, i, far_core_rows).wait_recv()
        for c in range(len(pieces)):
            rfwd(c, back).wait_recv()
        prepare(near_slot)

    relax_window(V1, V2, layer(2))

    @pl.when(flow)
    def _():
        relax_window(V1, V2, layer(1))

    restrict(2 + 2 * odd, base + odd)

    rview = lambda b: CR.at[pl.ds(b - lax.rem(b, 2), 2), coarse_rows_of(lax.rem(b, 2)), :]
    rgather = (rview, bzs, bps, br)
    gather_start(*rgather)

    def edge_copy(buf, ss, rs, d, dest):
        return remote(buf.at[2 + 3 * d], buf.at[6 - 5 * d], ss.at[d], rs.at[d], dest, j)

    def edges_start(buf, ss, rs):
        @pl.when(down)
        def _():
            edge_copy(buf, ss, rs, 0, below).start()

        @pl.when(up)
        def _():
            edge_copy(buf, ss, rs, 1, above).start()

    def edges_finish(buf, ss, rs):
        @pl.when(up)
        def _():
            edge_copy(buf, ss, rs, 0, above).wait_recv()

        @pl.when(down)
        def _():
            edge_copy(buf, ss, rs, 1, below).wait_recv()

    def edges_sent(buf, ss, rs):
        @pl.when(down)
        def _():
            edge_copy(buf, ss, rs, 0, below).wait_send()

        @pl.when(up)
        def _():
            edge_copy(buf, ss, rs, 1, above).wait_send()

    part = hy // 2
    cross = [(3, 0, part), (3, part, part), (4, 0, part), (4, part, part), (5 - 3 * odd, 0, hy), (6 - 5 * odd, 0, hy)]
    cross_in = [(3, 0, part), (3, part, part), (4, 0, part), (4, part, part), (5 - 3 * even, 0, hy), (6 - 5 * even, 0, hy)]

    def wsend(c):
        q, start, size = cross[c]
        return remote(
            W4.at[q, eight(lead + start, size), :], WX.at[q - 3 + 2 * odd, pl.ds(start, size), :], xs.at[c], xr.at[c], partner, j
        )

    def wrecv(c):
        q, start, size = cross_in[c]
        return remote(
            W4.at[q, eight(lead + start, size), :], WX.at[q - 1 - 2 * odd, pl.ds(start, size), :], xs.at[c], xr.at[c], partner, j
        )

    relax_window(V2, W3, 2)
    relax_window(V2, W3, 5)

    def third_middle(q, carry):
        relax_window(V2, W3, q)
        return carry

    lax.fori_loop(3, 5, third_middle, 0)

    def fourth_middle(q, carry):
        relax_window(W3, W4, q)
        return carry

    lax.fori_loop(3, 5, fourth_middle, 0)
    for c in range(3):
        wsend(c).start()
    cfar_copy(cfar).wait_recv()
    ccorefar_copy(cfar).start()
    gather_forward(*rgather)
    edges_start(W3, w3s, w3r)
    ccore_copy(ccore).wait_recv()
    ccorefar_copy(cfarcore).wait_recv()

    edge = hy // TILES
    lane_tile = iota((hz, hz), 0) // (hz // TILES) == iota((hz, hz), 1) // (hz // TILES)
    same_tile = lane_tile.astype(BF16)

    def lane_sums(x):
        return sum(dot(piece, same_tile) for piece in split(x, 3))

    bgf = bg_ref[...].astype(F32).astype(BF16)
    ids = []
    for ty in range(TILES):
        pick = iota((TILES * TILES, hz), 0) == ty * TILES + iota((TILES * TILES, hz), 1) // (hz // TILES)
        ids.append(dot(bgf, pick.astype(BF16)))

    brick_row = iota((n, hz), 0)
    lane = iota((n, hz), 1)
    tile_lanes = hz // TILES

    def lower_brick(x, fill):
        return jnp.where(brick_row == 0, fill, pltpu.roll(x, 1, 0))

    def upper_brick(x, fill):
        return jnp.where(brick_row == n - 1, fill, pltpu.roll(x, n - 1, 0))

    def group_sums(fields):
        out = []
        for ty in range(TILES):
            total = jnp.zeros((n, hz), F32)
            for b in range(n):
                total = total + jnp.where(ids[ty][b : b + 1] == ids[ty], fields[ty][b : b + 1], 0.0)
            out.append(total)
        return out

    def coarse_first(b, carry):
        d = DC[b]
        CI[b] = relax_fine / (d + 14.0 * kap1)
        for ty in range(TILES):
            DSUM[ty, pl.ds(b, 1), :] = jnp.sum(d[ty * edge : (ty + 1) * edge], axis=0, keepdims=True)
        return carry

    lax.fori_loop(0, n, coarse_first, 0)
    dens_sum = [lane_sums(DSUM[ty]) for ty in range(TILES)]
    weight = []
    for ty in range(TILES):
        fx = 1.0 + 0.5 * (lower_brick(ids[ty], -1.0) == ids[ty]).astype(F32)
        fx = fx + 0.5 * (upper_brick(ids[ty], -1.0) == ids[ty]).astype(F32)
        cells = edge * tile_lanes
        weight.append(16.0 * cells - 2.0 * (2 * edge - 1) * (2 * tile_lanes - 1) * fx)
    totals0 = group_sums(dens_sum)
    totals1 = group_sums(weight)
    step = [relax_coarse / (totals0[ty] + kap1 * totals1[ty]) for ty in range(TILES)]

    def invert(i, carry):
        IE[i] = relax_fine / (D[odd + i // 2, lax.rem(i, 2)] + 14.0 * kap)
        return carry

    lax.fori_loop(0, 6, invert, 0)
    edges_finish(W3, w3s, w3r)
    relax_window(W3, W4, 2)
    relax_window(W3, W4, 5)
    edges_start(W4, w4s, w4r)
    gather_finish(*rgather)
    wsend(3).start()
    wsend(4).start()

    def coarse_start(b, carry):
        CA[b + 1] = CR[b] * CI[b]
        return carry

    lax.fori_loop(0, n, coarse_start, 0)

    def coarse_defect(src, b):
        v = src[b + 1]
        f = stencil(src[b], v, src[b + 2])
        return v, CR[b] - (DC[b] + 16.0 * kap1) * v + 2.0 * kap1 * f

    def coarse_relax(src, dst):
        def body(b, carry):
            v = src[b + 1]
            f = stencil(src[b], v, src[b + 2])
            dst[b + 1] = (1.0 - relax_fine) * v + CI[b] * (CR[b] + 2.0 * kap1 * (f - v))
            return carry

        return body

    lax.fori_loop(0, n, coarse_relax(CA, CB), 0)

    def remainder(b, carry):
        defect = coarse_defect(CB, b)[1]
        for ty in range(TILES):
            RS[ty, pl.ds(b, 1), :] = jnp.sum(defect[ty * edge : (ty + 1) * edge], axis=0, keepdims=True)
        return carry

    lax.fori_loop(0, n, remainder, 0)
    group_rhs = group_sums([lane_sums(RS[ty]) for ty in range(TILES)])
    fix = [step[ty] * group_rhs[ty] for ty in range(TILES)]

    def aggregate_image(g):
        along = [x + 0.5 * (lower_brick(x, 0.0) + upper_brick(x, 0.0)) for x in g]
        blank = jnp.zeros((n, hz), F32)
        out = []
        for ty in range(TILES):
            below = along[ty - 1] if ty > 0 else blank
            above = along[ty + 1] if ty < TILES - 1 else blank
            mid = (2.0 * edge - 1.0) * along[ty] + 0.5 * (below + above)
            left = jnp.where(lane < tile_lanes, 0.0, pltpu.roll(mid, tile_lanes, 1))
            right = jnp.where(lane >= hz - tile_lanes, 0.0, pltpu.roll(mid, hz - tile_lanes, 1))
            f = (2.0 * tile_lanes - 1.0) * mid + 0.5 * (left + right)
            own = dens_sum[ty] + 16.0 * kap1 * (edge * tile_lanes)
            out.append(own * g[ty] - 2.0 * kap1 * f)
        return group_sums(out)

    for _ in range(COARSE_SWEEPS - 1):
        image = aggregate_image(fix)
        fix = [fix[ty] + step[ty] * (group_rhs[ty] - image[ty]) for ty in range(TILES)]
    for ty in range(TILES):
        FX[ty] = fix[ty]

    def add_fix(b, carry):
        for ty in range(TILES):
            part = pl.ds(ty * edge, edge)
            CA[b + 1, part, :] = CB[b + 1, part, :] + FX[ty, pl.ds(b, 1), :]
        return carry

    def near(width):
        return jnp.maximum(me - width, 0), jnp.minimum(me + width + 1, n)

    lax.fori_loop(*near(4), add_fix, 0)
    lax.fori_loop(*near(3), coarse_relax(CA, CB), 0)
    lax.fori_loop(*near(2), coarse_relax(CB, CA), 0)

    edges_finish(W4, w4s, w4r)
    wsend(5).start()

    def inside(e):
        g = 2 * me + e - 3
        return jnp.logical_and(g >= 0, g < 2 * n)

    for t in range(5):
        b = me + t - 2
        valid = jnp.logical_and(b >= 0, b < n)
        fine = jnp.where(valid, refine_layer(CA[jnp.clip(b, 0, n - 1) + 1]), 0.0)
        for e in (2 * t - 1, 2 * t):
            if 0 <= e < 8:
                S[e] = fine

    def relax_error(src, e):
        v = src[e]
        f = stencil(src[e - 1], v, src[e + 1])
        out = (1.0 - relax_fine) * v + IE[e - 1] * (2.0 * kap * (f - v))
        return jnp.where(inside(e), out, 0.0)

    def third(e, carry):
        E3[e] = relax_error(S, e)
        return carry

    lax.fori_loop(1, 7, third, 0)
    for c in range(6):
        wrecv(c).wait_recv()

    def fourth(e, carry):
        S[e] = relax_error(E3, e)
        q = e - 1 + 2 * odd
        S[e, my_half, :] = S[e, my_half, :] + W4[q, eight(lead, hy), :]
        S[e, their_half, :] = S[e, their_half, :] + WX[e - 2]
        return carry

    lax.fori_loop(2, 6, fourth, 0)

    def last(i, carry):
        v = S[i + 3]
        sol_ref[i] = v
        f = stencil(S[i + 2], v, S[i + 4])
        res_ref[i] = RF[i] - (D[mine, i] + 16.0 * kap) * v + 2.0 * kap * f
        return carry

    lax.fori_loop(0, 2, last, 0)

    for i in range(2):
        dpair(i, mine).wait_send()
    for c in range(len(pieces)):
        rpair(c, mine).wait_send()
    for kind in (0, 1):
        for i in range(2):
            dfar(kind, i, my_rows).wait_send()
            dcore(kind, i, my_rows).wait_send()
            dcorefar(kind, i, far_rows).wait_send()

    @pl.when(flow)
    def _():
        rback(back).wait_send()
        dback(back).wait_send()
        for i in range(2):
            dfar(2, i, my_rows).wait_send()
            dcore(2, i, my_rows).wait_send()
            dcorefar(2, i, far_rows).wait_send()

    @pl.when(fhigh)
    def _():
        dbackcore(lane_of).wait_send()
        for i in range(2):
            dfwd(i, onward).wait_send()
        for c in range(len(pieces)):
            rfwd(c, onward).wait_send()

    gather_sent(*dgather)
    gather_sent(*rgather)
    cfar_copy(cmine).wait_send()
    ccore_copy(cmine).wait_send()
    ccorefar_copy(cfar).wait_send()
    edges_sent(W3, w3s, w3r)
    edges_sent(W4, w4s, w4r)
    for c in range(6):
        wsend(c).wait_send()


def local(n, spec, rhs, density, kappa, block_group):
    _, cells, ny, nz = rhs.shape
    hy, hz = ny // 2, nz // 2
    window = hy + 8
    count = len(pieces_of(window))
    fine = lambda *lead: pltpu.VMEM(lead + (ny, nz), F32)
    strip = lambda *lead: pltpu.VMEM(lead + (window, nz), F32)
    coarse = lambda *lead: pltpu.VMEM(lead + (hy, hz), F32)
    dma = lambda *shape: pltpu.SemaphoreType.DMA(shape)
    vmem = pl.BlockSpec(memory_space=pltpu.VMEM)
    out = jax.ShapeDtypeStruct((cells, ny, nz), F32)
    hbm = lambda x: pltpu.with_memory_space_constraint(x, pltpu.HBM)
    sol, res = pl.pallas_call(
        functools.partial(kernel, n, spec),
        out_shape=(out, out),
        in_specs=[pl.BlockSpec(memory_space=pltpu.HBM)] * 4,
        out_specs=(vmem, vmem),
        scratch_shapes=[
            pltpu.SMEM((1,), F32), pltpu.VMEM(block_group.shape, jnp.int32),
            strip(8), fine(2), fine(4, 2), strip(8), fine(6), strip(8), strip(8), strip(8), strip(8),
            pltpu.VMEM((4, hy, nz), F32), fine(8), fine(8),
            coarse(n), coarse(n), coarse(n), coarse(n + 2), coarse(n + 2),
            pltpu.VMEM((TILES, n, hz), F32), pltpu.VMEM((TILES, n, hz), F32), pltpu.VMEM((TILES, n, hz), F32),
            dma(count), dma(count), dma(count), dma(count), dma(1), dma(1), dma(2, 2), dma(2, 2),
            dma(3, 3, 2), dma(3, 3, 2), dma(2), dma(2),
            dma(n // 2), dma(n // 2), dma(n), dma(3), dma(3),
            dma(n // 2), dma(n // 2), dma(n), dma(2), dma(2), dma(2), dma(2), dma(6), dma(6), dma(5),
        ],
        compiler_params=pltpu.CompilerParams(
            collective_id=0, has_side_effects=True, vmem_limit_bytes=(26 << 20) + 24 * n * hy * hz
        ),
    )(kappa, hbm(block_group), hbm(rhs.reshape(cells, ny, nz)), hbm(density))
    return sol[None], res[None]


def solution(mesh):
    return jax.shard_map(
        functools.partial(local, mesh.shape["brick"], mesh.shape["spec"]),
        mesh=mesh,
        in_specs=(P("spec", "brick", None, None), P("brick", "spec", None), P("spec"), P()),
        out_specs=(P("spec", "brick", None, None), P("spec", "brick", None, None)),
        check_vma=False,
    )
```

```python
import functools

import jax
import jax.numpy as jnp
from jax import lax
from jax.experimental import pallas as pl
from jax.experimental.pallas import tpu as pltpu
from jax.sharding import PartitionSpec as P

TILES = 4
COARSE_SWEEPS = 3
relax_fine = 0.85
relax_coarse = 0.6
MESH = pl.DeviceIdType.MESH
F32 = jnp.float32
BF16 = jnp.bfloat16


def iota(shape, dim):
    return lax.broadcasted_iota(jnp.int32, shape, dim)


def split(x, parts):
    out = []
    for _ in range(parts):
        piece = x.astype(BF16)
        out.append(piece)
        x = x - piece.astype(F32)
    return out


def dot(a, b):
    return jnp.dot(a, b, preferred_element_type=F32)


def filter_rows(m):
    size = m.shape[0]
    row = iota(m.shape, 0)
    before = jnp.where(row == 0, 0.0, pltpu.roll(m, 1, 0))
    after = jnp.where(row == size - 1, 0.0, pltpu.roll(m, size - 1, 0))
    return m + 0.5 * (before + after)


def filter_lanes(m):
    size = m.shape[1]
    lane = iota(m.shape, 1)
    before = jnp.where(lane == 0, 0.0, pltpu.roll(m, 1, 1))
    after = jnp.where(lane == size - 1, 0.0, pltpu.roll(m, size - 1, 1))
    return m + 0.5 * (before + after)


def stencil(low, mid, high):
    return filter_lanes(filter_rows(mid + 0.5 * (low + high)))


def pair_matrix(fine, coarse):
    return (iota((coarse, fine), 1) // 2 == iota((coarse, fine), 0)).astype(BF16)


def pair_matrix_t(fine, coarse):
    return (iota((fine, coarse), 0) // 2 == iota((fine, coarse), 1)).astype(BF16)


def coarsen_sum(x, left=None):
    rows, cols = x.shape
    if left is None:
        left = pair_matrix(rows, rows // 2)
    right = pair_matrix_t(cols, cols // 2)
    halves = sum(dot(left, piece) for piece in split(x, 2))
    return sum(dot(piece, right) for piece in split(halves, 2)) * 0.125


def pieces_of(rows):
    units = rows // 8
    sizes = [max(1, round(units * share)) for share in (0.3, 0.3, 0.22, 0.12)]
    sizes.append(units - sum(sizes))
    starts = [sum(sizes[:c]) for c in range(len(sizes))]
    return [(8 * start, 8 * size) for start, size in zip(starts, sizes)]


def refine_layer(c):
    rows, cols = c.shape
    left = pair_matrix_t(2 * rows, rows)
    right = pair_matrix(2 * cols, cols)
    total = None
    for piece in split(c, 2):
        term = dot(dot(left, piece).astype(BF16), right)
        total = term if total is None else total + term
    return total


def kernel(
    n, spec, kappa_hbm, bg_hbm, rhs_ref, dens_ref, out_ref,
    kappa_ref, bg_ref,
    R, RF, D, IW, IE, V1, V2, W3, W4, WX, S, E3, CR, DC, CI, CA, CB, RS, DSUM, FX,
    prs, prr, frs, frr, rgs, rgr, dss, dsr, gss, gsr, dgs, dgr,
    azs, aps, ar, ass, asr, bzs, bps, br, w3s, w3r, w4s, w4r, xs, xr, ls,
):
    me = lax.axis_index("brick")
    j = lax.axis_index("spec")
    odd = lax.rem(me, 2)
    even = 1 - odd
    base = me - odd
    partner = base + even
    ny, nz = rhs_ref.shape[1], rhs_ref.shape[2]
    hy, hz = ny // 2, nz // 2
    rows = dens_ref.shape[1]
    half = n // 2
    window = R.shape[1]
    pieces = pieces_of(window)
    down, up = base > 0, base + 2 < n
    flow = jnp.logical_or(jnp.logical_and(odd == 0, down), jnp.logical_and(odd == 1, up))
    fhigh = jnp.logical_or(jnp.logical_and(odd == 0, up), jnp.logical_and(odd == 1, down))
    onward = lax.rem(me + 2 - 4 * odd + n, n)
    back = lax.rem(me - 2 + 4 * odd + n, n)
    below = lax.rem(me - 2 + n, n)
    above = lax.rem(me + 2, n)
    core = j + 1 - 2 * lax.rem(j, 2)
    far = lax.rem(j + spec // 2, spec)
    mine, theirs, near_slot, far_slot = 1 + odd, 2 - odd, 3 * odd, 3 - 3 * odd

    def remote(src, dst, ssem, rsem, b, s):
        return pltpu.make_async_remote_copy(
            src_ref=src, dst_ref=dst, send_sem=ssem, recv_sem=rsem,
            device_id={"brick": b, "spec": s}, device_id_type=MESH,
        )

    barrier = pltpu.get_barrier_semaphore()
    for k in range(1, half):
        pl.semaphore_signal(barrier, inc=1, device_id={"brick": lax.rem(me + 2 * k, n), "spec": j}, device_id_type=MESH)
    pl.semaphore_signal(barrier, inc=1, device_id={"brick": partner, "spec": j}, device_id_type=MESH)
    pl.semaphore_signal(barrier, inc=1, device_id={"brick": me, "spec": core}, device_id_type=MESH)
    pl.semaphore_signal(barrier, inc=1, device_id={"brick": me, "spec": far}, device_id_type=MESH)

    def eight(start, size):
        return pl.ds(pl.multiple_of(start, 8), size)

    far_core = lax.rem(core + spec // 2, spec)
    my_rows, core_rows, far_rows, far_core_rows = [eight(at * rows, rows) for at in (j, core, far, far_core)]
    crows = rows // 2
    cmine, ccore, cfar, cfarcore = [eight(at * crows, crows) for at in (j, core, far, far_core)]
    win = odd * (ny - window)
    their_win = even * (ny - window)
    lead = 8 * odd
    my_half, their_half = eight(odd * hy, hy), eight(even * hy, hy)
    loads = [
        pltpu.make_async_copy(dens_ref, D.at[mine, :, my_rows, :], ls.at[0]),
        pltpu.make_async_copy(kappa_hbm, kappa_ref, ls.at[1]),
        pltpu.make_async_copy(bg_hbm, bg_ref, ls.at[2]),
        pltpu.make_async_copy(rhs_ref.at[:, eight(win, window), :], R.at[pl.ds(2 * mine, 2)], ls.at[3]),
        pltpu.make_async_copy(rhs_ref, RF, ls.at[4]),
    ]
    for load in loads:
        load.start()

    blank = jnp.zeros((window, nz), F32)

    @pl.when(jnp.logical_not(down))
    def _():
        for buf, q in ((V1, 0), (V1, 1), (V2, 1), (W3, 1), (W4, 1)):
            buf[q] = blank

    @pl.when(jnp.logical_not(up))
    def _():
        for buf, q in ((V1, 6), (V1, 7), (V2, 6), (W3, 6), (W4, 6)):
            buf[q] = blank

    zero = jnp.zeros((hy, hz), F32)
    for buf in (CA, CB):
        buf[0] = zero
        buf[n + 1] = zero
    for load in loads[:3]:
        load.wait()
    kap = kappa_ref[0]
    kap1 = 0.25 * kap
    DC[me, cmine, :] = coarsen_sum(D[mine, 0, my_rows, :] + D[mine, 1, my_rows, :])
    pl.semaphore_wait(barrier, half - 1 + 3)

    def dpair(i, slot):
        return remote(dens_ref.at[i], D.at[slot, i, my_rows, :], dss.at[0, i], dsr.at[0, i], partner, j)

    def dfwd(i, dest):
        return remote(D.at[theirs, i, my_rows, :], D.at[near_slot, i, my_rows, :], dss.at[1, i], dsr.at[1, i], dest, j)

    def rpair(c, slot):
        start, size = pieces[c]
        return remote(
            rhs_ref.at[:, eight(their_win + start, size), :], R.at[pl.ds(2 * slot, 2), pl.ds(start, size), :],
            prs.at[c], prr.at[c], partner, j,
        )

    def rfwd(c, dest):
        start, size = pieces[c]
        return remote(
            R.at[pl.ds(2 * theirs, 2), pl.ds(start, size), :], R.at[pl.ds(2 * near_slot, 2), pl.ds(start, size), :],
            frs.at[c], frr.at[c], dest, j,
        )

    def rback(dest):
        return remote(rhs_ref.at[:, eight(win, window), :], R.at[pl.ds(2 * far_slot, 2)], rgs.at[0], rgr.at[0], dest, j)

    slots = (mine, theirs, near_slot)

    def dsrc(kind, i):
        return dens_ref.at[i] if kind == 0 else D.at[slots[kind], i, my_rows, :]

    def dfar(kind, i, at):
        return remote(dsrc(kind, i), D.at[slots[kind], i, at, :], gss.at[kind, 0, i], gsr.at[kind, 0, i], me, far)

    def dcore(kind, i, at):
        return remote(dsrc(kind, i), D.at[slots[kind], i, at, :], gss.at[kind, 1, i], gsr.at[kind, 1, i], me, core)

    def dcorefar(kind, i, at):
        return remote(
            D.at[slots[kind], i, far_rows, :], D.at[slots[kind], i, at, :], gss.at[kind, 2, i], gsr.at[kind, 2, i], me, core
        )

    strip = (hy + 16) // 2
    strip_win = odd * (hy - 16)

    def strip_rows(which):
        return eight(strip_win + strip * which, strip)

    lane_of = lax.rem(j, 2)

    def dback(dest):
        at = strip_rows(lane_of)
        return remote(D.at[mine, :, at, :], D.at[far_slot, :, at, :], dgs.at[0], dgr.at[0], dest, j)

    def dbackcore(which):
        at = strip_rows(which)
        return remote(D.at[far_slot, :, at, :], D.at[far_slot, :, at, :], dgs.at[1], dgr.at[1], me, core)

    def gather_start(view, zs, ps, rs):
        for k in range(1, half):
            remote(view(me), view(me), zs.at[k], rs.at[me], lax.rem(me + 2 * k, n), j).start()
        remote(view(me), view(me), ps.at[0], rs.at[me], partner, j).start()

    def gather_forward(view, zs, ps, rs):
        for k in range(1, half):
            b = lax.rem(me + 2 * k, n)
            remote(view(b), view(b), zs.at[k], rs.at[b], partner, j).wait_recv()
            remote(view(b), view(b), ps.at[k], rs.at[b], partner, j).start()

    def gather_finish(view, zs, ps, rs):
        for k in range(half):
            b = lax.rem(partner + 2 * k, n)
            remote(view(b), view(b), ps.at[k], rs.at[b], partner, j).wait_recv()

    def gather_sent(view, zs, ps, rs):
        for k in range(1, half):
            remote(view(me), view(me), zs.at[k], rs.at[me], partner, j).wait_send()
        for k in range(half):
            remote(view(me), view(me), ps.at[k], rs.at[me], partner, j).wait_send()

    dview = lambda b: DC.at[b, cmine, :]
    dgather = (dview, azs, aps, ar)
    for i in range(2):
        dpair(i, mine).start()
    for i in range(2):
        dfar(0, i, my_rows).start()
        dcore(0, i, my_rows).start()

    @pl.when(flow)
    def _():
        rback(back).start()

    gather_start(*dgather)
    dpair(0, mine).wait_send()
    rpair(0, mine).start()
    dpair(1, mine).wait_send()
    for c in range(1, len(pieces)):
        rpair(c, mine).start()

    def cfar_copy(at):
        return remote(DC.at[:, cmine, :], DC.at[:, at, :], ass.at[0], asr.at[0], me, far)

    def ccore_copy(at):
        return remote(DC.at[:, cmine, :], DC.at[:, at, :], ass.at[1], asr.at[1], me, core)

    def ccorefar_copy(at):
        return remote(DC.at[:, cfar, :], DC.at[:, at, :], ass.at[2], asr.at[2], me, core)

    def pass_on(c):
        rpair(c, theirs).wait_recv()

        @pl.when(fhigh)
        def _():
            rfwd(c, onward).start()

    def prepare(slot):
        def body(i, carry):
            inv = relax_fine / (D[slot, i, eight(win, window), :] + 14.0 * kap)
            IW[2 * slot + i] = inv
            V1[2 * slot + i] = R[2 * slot + i] * inv
            return carry

        lax.fori_loop(0, 2, body, 0)

    def layer(k):
        return k + odd * (7 - 2 * k)

    def relax_window(src, dst, q):
        v = src[q]
        f = stencil(src[q - 1], v, src[q + 1])
        dst[q] = (1.0 - relax_fine) * v + IW[q] * (R[q] + 2.0 * kap * (f - v))

    def residual_window(q):
        v = V2[q]
        f = stencil(V2[q - 1], v, V2[q + 1])
        d = D[q // 2, lax.rem(q, 2), eight(win, window), :]
        return R[q] - (d + 16.0 * kap) * v + 2.0 * kap * f

    chalf = hy // 2
    pick = (iota((chalf, window), 1) // 2 - lead // 2 == iota((chalf, window), 0)).astype(BF16)

    def coarse_rows_of(parity):
        return eight(parity * chalf, chalf)

    def rview(side, b):
        return CR.at[b if side else b + 1 - 2 * lax.rem(b, 2), coarse_rows_of(lax.rem(b, 2)), :]

    rgathers = [(functools.partial(rview, side), bzs.at[side], bps.at[side], br.at[side]) for side in range(2)]

    def restrict(q, brick):
        CR[brick, coarse_rows_of(odd), :] = coarsen_sum(residual_window(q) + residual_window(q + 1), pick)

    loads[3].wait()
    loads[4].wait()
    for i in range(2):
        dpair(i, theirs).wait_recv()

        @pl.when(fhigh)
        def _():
            dfwd(i, onward).start()

        dfar(1, i, my_rows).start()
        dcore(1, i, my_rows).start()
        dfar(0, i, far_rows).wait_recv()
        dcorefar(0, i, far_rows).start()

    for i in range(2):
        dcore(0, i, core_rows).wait_recv()
        dcorefar(0, i, far_core_rows).wait_recv()

    @pl.when(flow)
    def _():
        dback(back).start()

    prepare(mine)
    pass_on(0)

    @pl.when(flow)
    def _():
        for i in range(2):
            dfwd(i, back).wait_recv()
            dfar(2, i, my_rows).start()
            dcore(2, i, my_rows).start()

    pass_on(1)
    for i in range(2):
        dfar(1, i, far_rows).wait_recv()
        dcorefar(1, i, far_rows).start()
    pass_on(2)
    gather_forward(*dgather)
    for c in range(3, len(pieces)):
        pass_on(c)

    @pl.when(fhigh)
    def _():
        dback(onward).wait_recv()
        dbackcore(lane_of).start()

    for i in range(2):
        dcore(1, i, core_rows).wait_recv()
        dcorefar(1, i, far_core_rows).wait_recv()
    prepare(theirs)
    for k in (3, 4):
        relax_window(V1, V2, layer(k))

    @pl.when(flow)
    def _():
        for i in range(2):
            dfar(2, i, far_rows).wait_recv()
            dcorefar(2, i, far_rows).start()

    @pl.when(fhigh)
    def _():
        rback(onward).wait_recv()
        dbackcore(1 - lane_of).wait_recv()
        prepare(far_slot)

    relax_window(V1, V2, layer(5))

    @pl.when(fhigh)
    def _():
        relax_window(V1, V2, layer(6))

    restrict(4 - 2 * odd, base + even)
    gather_start(*rgathers[0])
    gather_finish(*dgather)
    cfar_copy(cmine).start()
    ccore_copy(cmine).start()

    @pl.when(flow)
    def _():
        for i in range(2):
            dcore(2, i, core_rows).wait_recv()
            dcorefar(2, i, far_core_rows).wait_recv()
        for c in range(len(pieces)):
            rfwd(c, back).wait_recv()
        prepare(near_slot)

    relax_window(V1, V2, layer(2))

    @pl.when(flow)
    def _():
        relax_window(V1, V2, layer(1))

    restrict(2 + 2 * odd, base + odd)

    gather_start(*rgathers[1])

    def edge_copy(buf, ss, rs, d, dest):
        return remote(buf.at[2 + 3 * d], buf.at[6 - 5 * d], ss.at[d], rs.at[d], dest, j)

    def edges_start(buf, ss, rs):
        @pl.when(down)
        def _():
            edge_copy(buf, ss, rs, 0, below).start()

        @pl.when(up)
        def _():
            edge_copy(buf, ss, rs, 1, above).start()

    def edges_finish(buf, ss, rs):
        @pl.when(up)
        def _():
            edge_copy(buf, ss, rs, 0, above).wait_recv()

        @pl.when(down)
        def _():
            edge_copy(buf, ss, rs, 1, below).wait_recv()

    def edges_sent(buf, ss, rs):
        @pl.when(down)
        def _():
            edge_copy(buf, ss, rs, 0, below).wait_send()

        @pl.when(up)
        def _():
            edge_copy(buf, ss, rs, 1, above).wait_send()

    part = hy // 2
    cross = [(3, 0, part), (3, part, part), (4, 0, part), (4, part, part), (5 - 3 * odd, 0, hy), (6 - 5 * odd, 0, hy)]
    cross_in = [(3, 0, part), (3, part, part), (4, 0, part), (4, part, part), (5 - 3 * even, 0, hy), (6 - 5 * even, 0, hy)]

    def wsend(c):
        q, start, size = cross[c]
        return remote(
            W4.at[q, eight(lead + start, size), :], WX.at[q - 3 + 2 * odd, pl.ds(start, size), :], xs.at[c], xr.at[c], partner, j
        )

    def wrecv(c):
        q, start, size = cross_in[c]
        return remote(
            W4.at[q, eight(lead + start, size), :], WX.at[q - 1 - 2 * odd, pl.ds(start, size), :], xs.at[c], xr.at[c], partner, j
        )

    relax_window(V2, W3, 2)
    relax_window(V2, W3, 5)

    def third_middle(q, carry):
        relax_window(V2, W3, q)
        return carry

    lax.fori_loop(3, 5, third_middle, 0)

    def fourth_middle(q, carry):
        relax_window(W3, W4, q)
        return carry

    lax.fori_loop(3, 5, fourth_middle, 0)
    for c in range(3):
        wsend(c).start()
    cfar_copy(cfar).wait_recv()
    ccorefar_copy(cfar).start()
    for rgather in rgathers:
        gather_forward(*rgather)
    edges_start(W3, w3s, w3r)
    ccore_copy(ccore).wait_recv()
    ccorefar_copy(cfarcore).wait_recv()

    edge = hy // TILES
    lane_tile = iota((hz, hz), 0) // (hz // TILES) == iota((hz, hz), 1) // (hz // TILES)
    same_tile = lane_tile.astype(BF16)

    def lane_sums(x):
        return sum(dot(piece, same_tile) for piece in split(x, 3))

    bgf = bg_ref[...].astype(F32).astype(BF16)
    ids = []
    for ty in range(TILES):
        pick = iota((TILES * TILES, hz), 0) == ty * TILES + iota((TILES * TILES, hz), 1) // (hz // TILES)
        ids.append(dot(bgf, pick.astype(BF16)))

    brick_row = iota((n, hz), 0)
    lane = iota((n, hz), 1)
    tile_lanes = hz // TILES

    def lower_brick(x, fill):
        return jnp.where(brick_row == 0, fill, pltpu.roll(x, 1, 0))

    def upper_brick(x, fill):
        return jnp.where(brick_row == n - 1, fill, pltpu.roll(x, n - 1, 0))

    def group_sums(fields):
        out = []
        for ty in range(TILES):
            total = jnp.zeros((n, hz), F32)
            for b in range(n):
                total = total + jnp.where(ids[ty][b : b + 1] == ids[ty], fields[ty][b : b + 1], 0.0)
            out.append(total)
        return out

    def coarse_first(b, carry):
        d = DC[b]
        CI[b] = relax_fine / (d + 14.0 * kap1)
        for ty in range(TILES):
            DSUM[ty, pl.ds(b, 1), :] = jnp.sum(d[ty * edge : (ty + 1) * edge], axis=0, keepdims=True)
        return carry

    lax.fori_loop(0, n, coarse_first, 0)
    dens_sum = [lane_sums(DSUM[ty]) for ty in range(TILES)]
    weight = []
    for ty in range(TILES):
        fx = 1.0 + 0.5 * (lower_brick(ids[ty], -1.0) == ids[ty]).astype(F32)
        fx = fx + 0.5 * (upper_brick(ids[ty], -1.0) == ids[ty]).astype(F32)
        cells = edge * tile_lanes
        weight.append(16.0 * cells - 2.0 * (2 * edge - 1) * (2 * tile_lanes - 1) * fx)
    totals0 = group_sums(dens_sum)
    totals1 = group_sums(weight)
    step = [relax_coarse / (totals0[ty] + kap1 * totals1[ty]) for ty in range(TILES)]

    def invert(i, carry):
        IE[i] = relax_fine / (D[odd + i // 2, lax.rem(i, 2)] + 14.0 * kap)
        return carry

    lax.fori_loop(0, 6, invert, 0)
    edges_finish(W3, w3s, w3r)
    relax_window(W3, W4, 2)
    relax_window(W3, W4, 5)
    edges_start(W4, w4s, w4r)
    for rgather in rgathers:
        gather_finish(*rgather)
    wsend(3).start()
    wsend(4).start()

    def coarse_start(b, carry):
        CA[b + 1] = CR[b] * CI[b]
        return carry

    lax.fori_loop(0, n, coarse_start, 0)

    def coarse_defect(src, b):
        v = src[b + 1]
        f = stencil(src[b], v, src[b + 2])
        return v, CR[b] - (DC[b] + 16.0 * kap1) * v + 2.0 * kap1 * f

    def coarse_relax(src, dst):
        def body(b, carry):
            v = src[b + 1]
            f = stencil(src[b], v, src[b + 2])
            dst[b + 1] = (1.0 - relax_fine) * v + CI[b] * (CR[b] + 2.0 * kap1 * (f - v))
            return carry

        return body

    lax.fori_loop(0, n, coarse_relax(CA, CB), 0)

    def remainder(b, carry):
        defect = coarse_defect(CB, b)[1]
        for ty in range(TILES):
            RS[ty, pl.ds(b, 1), :] = jnp.sum(defect[ty * edge : (ty + 1) * edge], axis=0, keepdims=True)
        return carry

    lax.fori_loop(0, n, remainder, 0)
    group_rhs = group_sums([lane_sums(RS[ty]) for ty in range(TILES)])
    fix = [step[ty] * group_rhs[ty] for ty in range(TILES)]

    def aggregate_image(g):
        along = [x + 0.5 * (lower_brick(x, 0.0) + upper_brick(x, 0.0)) for x in g]
        blank = jnp.zeros((n, hz), F32)
        out = []
        for ty in range(TILES):
            below = along[ty - 1] if ty > 0 else blank
            above = along[ty + 1] if ty < TILES - 1 else blank
            mid = (2.0 * edge - 1.0) * along[ty] + 0.5 * (below + above)
            left = jnp.where(lane < tile_lanes, 0.0, pltpu.roll(mid, tile_lanes, 1))
            right = jnp.where(lane >= hz - tile_lanes, 0.0, pltpu.roll(mid, hz - tile_lanes, 1))
            f = (2.0 * tile_lanes - 1.0) * mid + 0.5 * (left + right)
            own = dens_sum[ty] + 16.0 * kap1 * (edge * tile_lanes)
            out.append(own * g[ty] - 2.0 * kap1 * f)
        return group_sums(out)

    for _ in range(COARSE_SWEEPS - 1):
        image = aggregate_image(fix)
        fix = [fix[ty] + step[ty] * (group_rhs[ty] - image[ty]) for ty in range(TILES)]
    for ty in range(TILES):
        FX[ty] = fix[ty]

    def add_fix(b, carry):
        for ty in range(TILES):
            part = pl.ds(ty * edge, edge)
            CA[b + 1, part, :] = CB[b + 1, part, :] + FX[ty, pl.ds(b, 1), :]
        return carry

    def near(width):
        return jnp.maximum(me - width, 0), jnp.minimum(me + width + 1, n)

    lax.fori_loop(*near(4), add_fix, 0)
    lax.fori_loop(*near(3), coarse_relax(CA, CB), 0)
    lax.fori_loop(*near(2), coarse_relax(CB, CA), 0)

    edges_finish(W4, w4s, w4r)
    wsend(5).start()

    def inside(e):
        g = 2 * me + e - 3
        return jnp.logical_and(g >= 0, g < 2 * n)

    for t in range(5):
        b = me + t - 2
        valid = jnp.logical_and(b >= 0, b < n)
        fine = jnp.where(valid, refine_layer(CA[jnp.clip(b, 0, n - 1) + 1]), 0.0)
        for e in (2 * t - 1, 2 * t):
            if 0 <= e < 8:
                S[e] = fine

    def relax_error(src, e):
        v = src[e]
        f = stencil(src[e - 1], v, src[e + 1])
        out = (1.0 - relax_fine) * v + IE[e - 1] * (2.0 * kap * (f - v))
        return jnp.where(inside(e), out, 0.0)

    def third(e, carry):
        E3[e] = relax_error(S, e)
        return carry

    lax.fori_loop(1, 7, third, 0)
    for c in range(6):
        wrecv(c).wait_recv()

    def fourth(e, carry):
        S[e] = relax_error(E3, e)
        q = e - 1 + 2 * odd
        S[e, my_half, :] = S[e, my_half, :] + W4[q, eight(lead, hy), :]
        S[e, their_half, :] = S[e, their_half, :] + WX[e - 2]
        return carry

    lax.fori_loop(2, 6, fourth, 0)

    def last(i, carry):
        v = S[i + 3]
        out_ref[0, i] = v
        f = stencil(S[i + 2], v, S[i + 4])
        out_ref[1, i] = RF[i] - (D[mine, i] + 16.0 * kap) * v + 2.0 * kap * f
        return carry

    lax.fori_loop(0, 2, last, 0)

    for c in range(len(pieces)):
        rpair(c, mine).wait_send()
    for kind in (0, 1):
        for i in range(2):
            dfar(kind, i, my_rows).wait_send()
            dcore(kind, i, my_rows).wait_send()
            dcorefar(kind, i, far_rows).wait_send()

    @pl.when(flow)
    def _():
        rback(back).wait_send()
        dback(back).wait_send()
        for i in range(2):
            dfar(2, i, my_rows).wait_send()
            dcore(2, i, my_rows).wait_send()
            dcorefar(2, i, far_rows).wait_send()

    @pl.when(fhigh)
    def _():
        dbackcore(lane_of).wait_send()
        for i in range(2):
            dfwd(i, onward).wait_send()
        for c in range(len(pieces)):
            rfwd(c, onward).wait_send()

    gather_sent(*dgather)
    for rgather in rgathers:
        gather_sent(*rgather)
    cfar_copy(cmine).wait_send()
    ccore_copy(cmine).wait_send()
    ccorefar_copy(cfar).wait_send()
    edges_sent(W3, w3s, w3r)
    edges_sent(W4, w4s, w4r)
    for c in range(6):
        wsend(c).wait_send()


def local(n, spec, rhs, density, kappa, block_group):
    _, cells, ny, nz = rhs.shape
    hy, hz = ny // 2, nz // 2
    window = hy + 8
    count = len(pieces_of(window))
    fine = lambda *lead: pltpu.VMEM(lead + (ny, nz), F32)
    strip = lambda *lead: pltpu.VMEM(lead + (window, nz), F32)
    coarse = lambda *lead: pltpu.VMEM(lead + (hy, hz), F32)
    dma = lambda *shape: pltpu.SemaphoreType.DMA(shape)
    vmem = pl.BlockSpec(memory_space=pltpu.VMEM)
    out = jax.ShapeDtypeStruct((2, cells, ny, nz), F32)
    hbm = lambda x: pltpu.with_memory_space_constraint(x, pltpu.HBM)
    both = pl.pallas_call(
        functools.partial(kernel, n, spec),
        out_shape=out,
        in_specs=[pl.BlockSpec(memory_space=pltpu.HBM)] * 4,
        out_specs=vmem,
        scratch_shapes=[
            pltpu.SMEM((1,), F32), pltpu.VMEM(block_group.shape, jnp.int32),
            strip(8), fine(2), fine(4, 2), strip(8), fine(6), strip(8), strip(8), strip(8), strip(8),
            pltpu.VMEM((4, hy, nz), F32), fine(8), fine(8),
            coarse(n), coarse(n), coarse(n), coarse(n + 2), coarse(n + 2),
            pltpu.VMEM((TILES, n, hz), F32), pltpu.VMEM((TILES, n, hz), F32), pltpu.VMEM((TILES, n, hz), F32),
            dma(count), dma(count), dma(count), dma(count), dma(1), dma(1), dma(2, 2), dma(2, 2),
            dma(3, 3, 2), dma(3, 3, 2), dma(2), dma(2),
            dma(n // 2), dma(n // 2), dma(n), dma(3), dma(3),
            dma(2, n // 2), dma(2, n // 2), dma(2, n), dma(2), dma(2), dma(2), dma(2), dma(6), dma(6), dma(5),
        ],
        compiler_params=pltpu.CompilerParams(
            collective_id=0, has_side_effects=True, vmem_limit_bytes=(26 << 20) + 24 * n * hy * hz
        ),
    )(kappa, hbm(block_group), hbm(rhs.reshape(cells, ny, nz)), hbm(density))
    return both[:1], both[1:]


def solution(mesh):
    return jax.shard_map(
        functools.partial(local, mesh.shape["brick"], mesh.shape["spec"]),
        mesh=mesh,
        in_specs=(P("spec", "brick", None, None), P("brick", "spec", None), P("spec"), P()),
        out_specs=(P("spec", "brick", None, None), P("spec", "brick", None, None)),
        check_vma=False,
    )
```

```python
import functools

import jax
import jax.numpy as jnp
from jax import lax
from jax.experimental import pallas as pl
from jax.experimental.pallas import tpu as pltpu
from jax.sharding import PartitionSpec as P

TILES = 4
COARSE_SWEEPS = 3
relax_fine = 0.85
relax_coarse = 0.6
MESH = pl.DeviceIdType.MESH
F32 = jnp.float32
BF16 = jnp.bfloat16


def iota(shape, dim):
    return lax.broadcasted_iota(jnp.int32, shape, dim)


def split(x, parts):
    out = []
    for _ in range(parts):
        piece = x.astype(BF16)
        out.append(piece)
        x = x - piece.astype(F32)
    return out


def dot(a, b):
    return jnp.dot(a, b, preferred_element_type=F32)


def filter_rows(m):
    size = m.shape[0]
    row = iota(m.shape, 0)
    before = jnp.where(row == 0, 0.0, pltpu.roll(m, 1, 0))
    after = jnp.where(row == size - 1, 0.0, pltpu.roll(m, size - 1, 0))
    return m + 0.5 * (before + after)


def filter_lanes(m):
    size = m.shape[1]
    lane = iota(m.shape, 1)
    before = jnp.where(lane == 0, 0.0, pltpu.roll(m, 1, 1))
    after = jnp.where(lane == size - 1, 0.0, pltpu.roll(m, size - 1, 1))
    return m + 0.5 * (before + after)


def stencil(low, mid, high):
    return filter_lanes(filter_rows(mid + 0.5 * (low + high)))


def pair_matrix(fine, coarse):
    return (iota((coarse, fine), 1) // 2 == iota((coarse, fine), 0)).astype(BF16)


def pair_matrix_t(fine, coarse):
    return (iota((fine, coarse), 0) // 2 == iota((fine, coarse), 1)).astype(BF16)


def coarsen_sum(x, left=None):
    rows, cols = x.shape
    if left is None:
        left = pair_matrix(rows, rows // 2)
    right = pair_matrix_t(cols, cols // 2)
    halves = sum(dot(left, piece) for piece in split(x, 2))
    return sum(dot(piece, right) for piece in split(halves, 2)) * 0.125


def pieces_of(rows):
    units = rows // 8
    sizes = [max(1, round(units * share)) for share in (0.3, 0.3, 0.22, 0.12)]
    sizes.append(units - sum(sizes))
    starts = [sum(sizes[:c]) for c in range(len(sizes))]
    return [(8 * start, 8 * size) for start, size in zip(starts, sizes)]


def refine_layer(c):
    rows, cols = c.shape
    left = pair_matrix_t(2 * rows, rows)
    right = pair_matrix(2 * cols, cols)
    total = None
    for piece in split(c, 2):
        term = dot(dot(left, piece).astype(BF16), right)
        total = term if total is None else total + term
    return total


def kernel(
    n, spec, kappa_hbm, bg_hbm, rhs_ref, dens_ref, out_ref,
    kappa_ref, bg_ref,
    R, RF, D, IW, IE, V1, V2, W3, W4, WX, S, E3, CR, DC, CI, CA, CB, RS, DSUM, FX,
    prs, prr, frs, frr, rgs, rgr, dss, dsr, gss, gsr, dgs, dgr,
    azs, aps, ar, ass, asr, bzs, bps, br, w3s, w3r, w4s, w4r, xs, xr, ls,
):
    me = lax.axis_index("brick")
    j = lax.axis_index("spec")
    odd = lax.rem(me, 2)
    even = 1 - odd
    base = me - odd
    partner = base + even
    ny, nz = rhs_ref.shape[1], rhs_ref.shape[2]
    hy, hz = ny // 2, nz // 2
    rows = dens_ref.shape[1]
    half = n // 2
    window = R.shape[1]
    pieces = pieces_of(window)
    down, up = base > 0, base + 2 < n
    flow = jnp.logical_or(jnp.logical_and(odd == 0, down), jnp.logical_and(odd == 1, up))
    fhigh = jnp.logical_or(jnp.logical_and(odd == 0, up), jnp.logical_and(odd == 1, down))
    onward = lax.rem(me + 2 - 4 * odd + n, n)
    back = lax.rem(me - 2 + 4 * odd + n, n)
    below = lax.rem(me - 2 + n, n)
    above = lax.rem(me + 2, n)
    core = j + 1 - 2 * lax.rem(j, 2)
    far = lax.rem(j + spec // 2, spec)
    mine, theirs, near_slot, far_slot = 1 + odd, 2 - odd, 3 * odd, 3 - 3 * odd

    def remote(src, dst, ssem, rsem, b, s):
        return pltpu.make_async_remote_copy(
            src_ref=src, dst_ref=dst, send_sem=ssem, recv_sem=rsem,
            device_id={"brick": b, "spec": s}, device_id_type=MESH,
        )

    barrier = pltpu.get_barrier_semaphore()
    for k in range(1, half):
        pl.semaphore_signal(barrier, inc=1, device_id={"brick": lax.rem(me + 2 * k, n), "spec": j}, device_id_type=MESH)
    pl.semaphore_signal(barrier, inc=1, device_id={"brick": partner, "spec": j}, device_id_type=MESH)
    pl.semaphore_signal(barrier, inc=1, device_id={"brick": me, "spec": core}, device_id_type=MESH)
    pl.semaphore_signal(barrier, inc=1, device_id={"brick": me, "spec": far}, device_id_type=MESH)

    def eight(start, size):
        return pl.ds(pl.multiple_of(start, 8), size)

    far_core = lax.rem(core + spec // 2, spec)
    my_rows, core_rows, far_rows, far_core_rows = [eight(at * rows, rows) for at in (j, core, far, far_core)]
    crows = rows // 2
    cmine, ccore, cfar, cfarcore = [eight(at * crows, crows) for at in (j, core, far, far_core)]
    win = odd * (ny - window)
    their_win = even * (ny - window)
    lead = 8 * odd
    my_half, their_half = eight(odd * hy, hy), eight(even * hy, hy)
    loads = [
        pltpu.make_async_copy(dens_ref, D.at[mine, :, my_rows, :], ls.at[0]),
        pltpu.make_async_copy(kappa_hbm, kappa_ref, ls.at[1]),
        pltpu.make_async_copy(bg_hbm, bg_ref, ls.at[2]),
        pltpu.make_async_copy(rhs_ref.at[:, eight(win, window), :], R.at[pl.ds(2 * mine, 2)], ls.at[3]),
        pltpu.make_async_copy(rhs_ref, RF, ls.at[4]),
    ]
    for load in loads:
        load.start()

    blank = jnp.zeros((window, nz), F32)

    @pl.when(jnp.logical_not(down))
    def _():
        for buf, q in ((V1, 0), (V1, 1), (V2, 1), (W3, 1), (W4, 1)):
            buf[q] = blank

    @pl.when(jnp.logical_not(up))
    def _():
        for buf, q in ((V1, 6), (V1, 7), (V2, 6), (W3, 6), (W4, 6)):
            buf[q] = blank

    @pl.when(jnp.logical_not(flow))
    def _():
        WX[3 * odd] = jnp.zeros((hy, nz), F32)

    zero = jnp.zeros((hy, hz), F32)
    for buf in (CA, CB):
        buf[0] = zero
        buf[n + 1] = zero
    for load in loads[:3]:
        load.wait()
    kap = kappa_ref[0]
    kap1 = 0.25 * kap
    DC[me, cmine, :] = coarsen_sum(D[mine, 0, my_rows, :] + D[mine, 1, my_rows, :])
    pl.semaphore_wait(barrier, half - 1 + 3)

    def dpair(i, slot):
        return remote(dens_ref.at[i], D.at[slot, i, my_rows, :], dss.at[0, i], dsr.at[0, i], partner, j)

    def dfwd(i, dest):
        return remote(D.at[theirs, i, my_rows, :], D.at[near_slot, i, my_rows, :], dss.at[1, i], dsr.at[1, i], dest, j)

    def rpair(c, slot):
        start, size = pieces[c]
        return remote(
            rhs_ref.at[:, eight(their_win + start, size), :], R.at[pl.ds(2 * slot, 2), pl.ds(start, size), :],
            prs.at[c], prr.at[c], partner, j,
        )

    def rfwd(c, dest):
        start, size = pieces[c]
        return remote(
            R.at[pl.ds(2 * theirs, 2), pl.ds(start, size), :], R.at[pl.ds(2 * near_slot, 2), pl.ds(start, size), :],
            frs.at[c], frr.at[c], dest, j,
        )

    def rback(dest):
        return remote(rhs_ref.at[:, eight(win, window), :], R.at[pl.ds(2 * far_slot, 2)], rgs.at[0], rgr.at[0], dest, j)

    slots = (mine, theirs, near_slot)

    def dsrc(kind, i):
        return dens_ref.at[i] if kind == 0 else D.at[slots[kind], i, my_rows, :]

    def dfar(kind, i, at):
        return remote(dsrc(kind, i), D.at[slots[kind], i, at, :], gss.at[kind, 0, i], gsr.at[kind, 0, i], me, far)

    def dcore(kind, i, at):
        return remote(dsrc(kind, i), D.at[slots[kind], i, at, :], gss.at[kind, 1, i], gsr.at[kind, 1, i], me, core)

    def dcorefar(kind, i, at):
        return remote(
            D.at[slots[kind], i, far_rows, :], D.at[slots[kind], i, at, :], gss.at[kind, 2, i], gsr.at[kind, 2, i], me, core
        )

    strip = (hy + 16) // 2
    strip_win = odd * (hy - 16)

    def strip_rows(which):
        return eight(strip_win + strip * which, strip)

    lane_of = lax.rem(j, 2)

    def dback(dest):
        at = strip_rows(lane_of)
        return remote(D.at[mine, :, at, :], D.at[far_slot, :, at, :], dgs.at[0], dgr.at[0], dest, j)

    def dbackcore(which):
        at = strip_rows(which)
        return remote(D.at[far_slot, :, at, :], D.at[far_slot, :, at, :], dgs.at[1], dgr.at[1], me, core)

    def gather_start(view, zs, ps, rs):
        for k in range(1, half):
            remote(view(me), view(me), zs.at[k], rs.at[me], lax.rem(me + 2 * k, n), j).start()
        remote(view(me), view(me), ps.at[0], rs.at[me], partner, j).start()

    def gather_forward(view, zs, ps, rs):
        for k in range(1, half):
            b = lax.rem(me + 2 * k, n)
            remote(view(b), view(b), zs.at[k], rs.at[b], partner, j).wait_recv()
            remote(view(b), view(b), ps.at[k], rs.at[b], partner, j).start()

    def gather_finish(view, zs, ps, rs):
        for k in range(half):
            b = lax.rem(partner + 2 * k, n)
            remote(view(b), view(b), ps.at[k], rs.at[b], partner, j).wait_recv()

    def gather_sent(view, zs, ps, rs):
        for k in range(1, half):
            remote(view(me), view(me), zs.at[k], rs.at[me], partner, j).wait_send()
        for k in range(half):
            remote(view(me), view(me), ps.at[k], rs.at[me], partner, j).wait_send()

    dview = lambda b: DC.at[b, cmine, :]
    dgather = (dview, azs, aps, ar)
    for i in range(2):
        dpair(i, mine).start()
    for i in range(2):
        dfar(0, i, my_rows).start()
        dcore(0, i, my_rows).start()

    @pl.when(flow)
    def _():
        rback(back).start()

    gather_start(*dgather)
    dpair(0, mine).wait_send()
    rpair(0, mine).start()
    dpair(1, mine).wait_send()
    for c in range(1, len(pieces)):
        rpair(c, mine).start()

    def cfar_copy(at):
        return remote(DC.at[:, cmine, :], DC.at[:, at, :], ass.at[0], asr.at[0], me, far)

    def ccore_copy(at):
        return remote(DC.at[:, cmine, :], DC.at[:, at, :], ass.at[1], asr.at[1], me, core)

    def ccorefar_copy(at):
        return remote(DC.at[:, cfar, :], DC.at[:, at, :], ass.at[2], asr.at[2], me, core)

    def pass_on(c):
        rpair(c, theirs).wait_recv()

        @pl.when(fhigh)
        def _():
            rfwd(c, onward).start()

    def prepare(slot):
        def body(i, carry):
            inv = relax_fine / (D[slot, i, eight(win, window), :] + 14.0 * kap)
            IW[2 * slot + i] = inv
            V1[2 * slot + i] = R[2 * slot + i] * inv
            return carry

        lax.fori_loop(0, 2, body, 0)

    def layer(k):
        return k + odd * (7 - 2 * k)

    def relax_window(src, dst, q):
        v = src[q]
        f = stencil(src[q - 1], v, src[q + 1])
        dst[q] = (1.0 - relax_fine) * v + IW[q] * (R[q] + 2.0 * kap * (f - v))

    def residual_window(q):
        v = V2[q]
        f = stencil(V2[q - 1], v, V2[q + 1])
        d = D[q // 2, lax.rem(q, 2), eight(win, window), :]
        return R[q] - (d + 16.0 * kap) * v + 2.0 * kap * f

    chalf = hy // 2
    pick = (iota((chalf, window), 1) // 2 - lead // 2 == iota((chalf, window), 0)).astype(BF16)

    def coarse_rows_of(parity):
        return eight(parity * chalf, chalf)

    def rview(side, b):
        return CR.at[b if side else b + 1 - 2 * lax.rem(b, 2), coarse_rows_of(lax.rem(b, 2)), :]

    rgathers = [(functools.partial(rview, side), bzs.at[side], bps.at[side], br.at[side]) for side in range(2)]

    def restrict(q, brick):
        CR[brick, coarse_rows_of(odd), :] = coarsen_sum(residual_window(q) + residual_window(q + 1), pick)

    loads[3].wait()
    loads[4].wait()
    for i in range(2):
        dpair(i, theirs).wait_recv()

        @pl.when(fhigh)
        def _():
            dfwd(i, onward).start()

        dfar(1, i, my_rows).start()
        dcore(1, i, my_rows).start()
        dfar(0, i, far_rows).wait_recv()
        dcorefar(0, i, far_rows).start()

    for i in range(2):
        dcore(0, i, core_rows).wait_recv()
        dcorefar(0, i, far_core_rows).wait_recv()

    @pl.when(flow)
    def _():
        dback(back).start()

    prepare(mine)
    pass_on(0)

    @pl.when(flow)
    def _():
        for i in range(2):
            dfwd(i, back).wait_recv()
            dfar(2, i, my_rows).start()
            dcore(2, i, my_rows).start()

    pass_on(1)
    for i in range(2):
        dfar(1, i, far_rows).wait_recv()
        dcorefar(1, i, far_rows).start()
    pass_on(2)
    gather_forward(*dgather)
    for c in range(3, len(pieces)):
        pass_on(c)

    @pl.when(fhigh)
    def _():
        dback(onward).wait_recv()
        dbackcore(lane_of).start()

    for i in range(2):
        dcore(1, i, core_rows).wait_recv()
        dcorefar(1, i, far_core_rows).wait_recv()
    prepare(theirs)
    for k in (3, 4):
        relax_window(V1, V2, layer(k))

    @pl.when(flow)
    def _():
        for i in range(2):
            dfar(2, i, far_rows).wait_recv()
            dcorefar(2, i, far_rows).start()

    @pl.when(fhigh)
    def _():
        rback(onward).wait_recv()
        dbackcore(1 - lane_of).wait_recv()
        prepare(far_slot)

    relax_window(V1, V2, layer(5))

    @pl.when(fhigh)
    def _():
        relax_window(V1, V2, layer(6))

    restrict(4 - 2 * odd, base + even)
    gather_start(*rgathers[0])
    gather_finish(*dgather)
    cfar_copy(cmine).start()
    ccore_copy(cmine).start()

    @pl.when(flow)
    def _():
        for i in range(2):
            dcore(2, i, core_rows).wait_recv()
            dcorefar(2, i, far_core_rows).wait_recv()
        for c in range(len(pieces)):
            rfwd(c, back).wait_recv()
        prepare(near_slot)

    relax_window(V1, V2, layer(2))

    @pl.when(flow)
    def _():
        relax_window(V1, V2, layer(1))

    restrict(2 + 2 * odd, base + odd)

    gather_start(*rgathers[1])

    def edge_copy(buf, ss, rs, d, dest):
        return remote(buf.at[2 + 3 * d], buf.at[6 - 5 * d], ss.at[d], rs.at[d], dest, j)

    def edges_start(buf, ss, rs):
        @pl.when(down)
        def _():
            edge_copy(buf, ss, rs, 0, below).start()

        @pl.when(up)
        def _():
            edge_copy(buf, ss, rs, 1, above).start()

    def edges_finish(buf, ss, rs):
        @pl.when(up)
        def _():
            edge_copy(buf, ss, rs, 0, above).wait_recv()

        @pl.when(down)
        def _():
            edge_copy(buf, ss, rs, 1, below).wait_recv()

    def edges_sent(buf, ss, rs):
        @pl.when(down)
        def _():
            edge_copy(buf, ss, rs, 0, below).wait_send()

        @pl.when(up)
        def _():
            edge_copy(buf, ss, rs, 1, above).wait_send()

    part = hy // 2
    cross = [(3, 0, part), (3, part, part), (4, 0, part), (4, part, part), (5 - 3 * odd, 0, hy), (6 - 5 * odd, 0, hy)]
    cross_in = [(3, 0, part), (3, part, part), (4, 0, part), (4, part, part), (5 - 3 * even, 0, hy), (6 - 5 * even, 0, hy)]

    def wsend(c):
        q, start, size = cross[c]
        return remote(
            W4.at[q, eight(lead + start, size), :], WX.at[q - 3 + 2 * odd, pl.ds(start, size), :], xs.at[c], xr.at[c], partner, j
        )

    def wrecv(c):
        q, start, size = cross_in[c]
        return remote(
            W4.at[q, eight(lead + start, size), :], WX.at[q - 1 - 2 * odd, pl.ds(start, size), :], xs.at[c], xr.at[c], partner, j
        )

    relax_window(V2, W3, 2)
    relax_window(V2, W3, 5)

    def third_middle(q, carry):
        relax_window(V2, W3, q)
        return carry

    lax.fori_loop(3, 5, third_middle, 0)

    def fourth_middle(q, carry):
        relax_window(W3, W4, q)
        return carry

    lax.fori_loop(3, 5, fourth_middle, 0)
    for c in range(3):
        wsend(c).start()
    cfar_copy(cfar).wait_recv()
    ccorefar_copy(cfar).start()
    for rgather in rgathers:
        gather_forward(*rgather)
    edges_start(W3, w3s, w3r)
    ccore_copy(ccore).wait_recv()
    ccorefar_copy(cfarcore).wait_recv()

    edge = hy // TILES
    lane_tile = iota((hz, hz), 0) // (hz // TILES) == iota((hz, hz), 1) // (hz // TILES)
    same_tile = lane_tile.astype(BF16)

    def lane_sums(x):
        return sum(dot(piece, same_tile) for piece in split(x, 3))

    bgf = bg_ref[...].astype(F32).astype(BF16)
    ids = []
    for ty in range(TILES):
        pick = iota((TILES * TILES, hz), 0) == ty * TILES + iota((TILES * TILES, hz), 1) // (hz // TILES)
        ids.append(dot(bgf, pick.astype(BF16)))

    brick_row = iota((n, hz), 0)
    lane = iota((n, hz), 1)
    tile_lanes = hz // TILES

    def lower_brick(x, fill):
        return jnp.where(brick_row == 0, fill, pltpu.roll(x, 1, 0))

    def upper_brick(x, fill):
        return jnp.where(brick_row == n - 1, fill, pltpu.roll(x, n - 1, 0))

    def group_sums(fields):
        out = []
        for ty in range(TILES):
            total = jnp.zeros((n, hz), F32)
            for b in range(n):
                total = total + jnp.where(ids[ty][b : b + 1] == ids[ty], fields[ty][b : b + 1], 0.0)
            out.append(total)
        return out

    def coarse_first(b, carry):
        d = DC[b]
        CI[b] = relax_fine / (d + 14.0 * kap1)
        for ty in range(TILES):
            DSUM[ty, pl.ds(b, 1), :] = jnp.sum(d[ty * edge : (ty + 1) * edge], axis=0, keepdims=True)
        return carry

    lax.fori_loop(0, n, coarse_first, 0)
    dens_sum = [lane_sums(DSUM[ty]) for ty in range(TILES)]
    weight = []
    for ty in range(TILES):
        fx = 1.0 + 0.5 * (lower_brick(ids[ty], -1.0) == ids[ty]).astype(F32)
        fx = fx + 0.5 * (upper_brick(ids[ty], -1.0) == ids[ty]).astype(F32)
        cells = edge * tile_lanes
        weight.append(16.0 * cells - 2.0 * (2 * edge - 1) * (2 * tile_lanes - 1) * fx)
    totals0 = group_sums(dens_sum)
    totals1 = group_sums(weight)
    step = [relax_coarse / (totals0[ty] + kap1 * totals1[ty]) for ty in range(TILES)]

    def invert(i, carry):
        IE[i] = relax_fine / (D[odd + i // 2, lax.rem(i, 2)] + 14.0 * kap)
        return carry

    lax.fori_loop(0, 6, invert, 0)
    edges_finish(W3, w3s, w3r)
    relax_window(W3, W4, 2)
    relax_window(W3, W4, 5)
    edges_start(W4, w4s, w4r)
    for rgather in rgathers:
        gather_finish(*rgather)
    wsend(3).start()
    wsend(4).start()

    def coarse_start(b, carry):
        CA[b + 1] = CR[b] * CI[b]
        return carry

    lax.fori_loop(0, n, coarse_start, 0)

    def coarse_defect(src, b):
        v = src[b + 1]
        f = stencil(src[b], v, src[b + 2])
        return v, CR[b] - (DC[b] + 16.0 * kap1) * v + 2.0 * kap1 * f

    def coarse_relax(src, dst):
        def body(b, carry):
            v = src[b + 1]
            f = stencil(src[b], v, src[b + 2])
            dst[b + 1] = (1.0 - relax_fine) * v + CI[b] * (CR[b] + 2.0 * kap1 * (f - v))
            return carry

        return body

    lax.fori_loop(0, n, coarse_relax(CA, CB), 0)

    def remainder(b, carry):
        defect = coarse_defect(CB, b)[1]
        for ty in range(TILES):
            RS[ty, pl.ds(b, 1), :] = jnp.sum(defect[ty * edge : (ty + 1) * edge], axis=0, keepdims=True)
        return carry

    lax.fori_loop(0, n, remainder, 0)
    group_rhs = group_sums([lane_sums(RS[ty]) for ty in range(TILES)])
    fix = [step[ty] * group_rhs[ty] for ty in range(TILES)]

    def aggregate_image(g):
        along = [x + 0.5 * (lower_brick(x, 0.0) + upper_brick(x, 0.0)) for x in g]
        blank = jnp.zeros((n, hz), F32)
        out = []
        for ty in range(TILES):
            below = along[ty - 1] if ty > 0 else blank
            above = along[ty + 1] if ty < TILES - 1 else blank
            mid = (2.0 * edge - 1.0) * along[ty] + 0.5 * (below + above)
            left = jnp.where(lane < tile_lanes, 0.0, pltpu.roll(mid, tile_lanes, 1))
            right = jnp.where(lane >= hz - tile_lanes, 0.0, pltpu.roll(mid, hz - tile_lanes, 1))
            f = (2.0 * tile_lanes - 1.0) * mid + 0.5 * (left + right)
            own = dens_sum[ty] + 16.0 * kap1 * (edge * tile_lanes)
            out.append(own * g[ty] - 2.0 * kap1 * f)
        return group_sums(out)

    for _ in range(COARSE_SWEEPS - 1):
        image = aggregate_image(fix)
        fix = [fix[ty] + step[ty] * (group_rhs[ty] - image[ty]) for ty in range(TILES)]
    for ty in range(TILES):
        FX[ty] = fix[ty]

    def add_fix(b, carry):
        for ty in range(TILES):
            part = pl.ds(ty * edge, edge)
            CA[b + 1, part, :] = CB[b + 1, part, :] + FX[ty, pl.ds(b, 1), :]
        return carry

    def near(width):
        return jnp.maximum(me - width, 0), jnp.minimum(me + width + 1, n)

    lax.fori_loop(*near(4), add_fix, 0)
    lax.fori_loop(*near(3), coarse_relax(CA, CB), 0)
    lax.fori_loop(*near(2), coarse_relax(CB, CA), 0)

    edges_finish(W4, w4s, w4r)

    @pl.when(fhigh)
    def _():
        wsend(5).start()

    def inside(e):
        g = 2 * me + e - 3
        return jnp.logical_and(g >= 0, g < 2 * n)

    for t in range(5):
        b = me + t - 2
        valid = jnp.logical_and(b >= 0, b < n)
        fine = jnp.where(valid, refine_layer(CA[jnp.clip(b, 0, n - 1) + 1]), 0.0)
        for e in (2 * t - 1, 2 * t):
            if 0 <= e < 8:
                S[e] = fine

    def relax_error(src, e):
        v = src[e]
        f = stencil(src[e - 1], v, src[e + 1])
        out = (1.0 - relax_fine) * v + IE[e - 1] * (2.0 * kap * (f - v))
        return jnp.where(inside(e), out, 0.0)

    def third(e, carry):
        E3[e] = relax_error(S, e)
        return carry

    lax.fori_loop(1, 7, third, 0)
    for c in range(5):
        wrecv(c).wait_recv()

    @pl.when(flow)
    def _():
        wrecv(5).wait_recv()

    def fourth(e, carry):
        S[e] = relax_error(E3, e)
        q = e - 1 + 2 * odd
        S[e, my_half, :] = S[e, my_half, :] + W4[q, eight(lead, hy), :]
        S[e, their_half, :] = S[e, their_half, :] + WX[e - 2]
        return carry

    lax.fori_loop(2, 6, fourth, 0)

    def last(i, carry):
        v = S[i + 3]
        out_ref[0, i] = v
        f = stencil(S[i + 2], v, S[i + 4])
        out_ref[1, i] = RF[i] - (D[mine, i] + 16.0 * kap) * v + 2.0 * kap * f
        return carry

    lax.fori_loop(0, 2, last, 0)

    for c in range(len(pieces)):
        rpair(c, mine).wait_send()
    for kind in (0, 1):
        for i in range(2):
            dfar(kind, i, my_rows).wait_send()
            dcore(kind, i, my_rows).wait_send()
            dcorefar(kind, i, far_rows).wait_send()

    @pl.when(flow)
    def _():
        rback(back).wait_send()
        dback(back).wait_send()
        for i in range(2):
            dfar(2, i, my_rows).wait_send()
            dcore(2, i, my_rows).wait_send()
            dcorefar(2, i, far_rows).wait_send()

    @pl.when(fhigh)
    def _():
        dbackcore(lane_of).wait_send()
        for i in range(2):
            dfwd(i, onward).wait_send()
        for c in range(len(pieces)):
            rfwd(c, onward).wait_send()

    gather_sent(*dgather)
    for rgather in rgathers:
        gather_sent(*rgather)
    cfar_copy(cmine).wait_send()
    ccore_copy(cmine).wait_send()
    ccorefar_copy(cfar).wait_send()
    edges_sent(W3, w3s, w3r)
    edges_sent(W4, w4s, w4r)
    for c in range(5):
        wsend(c).wait_send()

    @pl.when(fhigh)
    def _():
        wsend(5).wait_send()


def local(n, spec, rhs, density, kappa, block_group):
    _, cells, ny, nz = rhs.shape
    hy, hz = ny // 2, nz // 2
    window = hy + 8
    count = len(pieces_of(window))
    fine = lambda *lead: pltpu.VMEM(lead + (ny, nz), F32)
    strip = lambda *lead: pltpu.VMEM(lead + (window, nz), F32)
    coarse = lambda *lead: pltpu.VMEM(lead + (hy, hz), F32)
    dma = lambda *shape: pltpu.SemaphoreType.DMA(shape)
    vmem = pl.BlockSpec(memory_space=pltpu.VMEM)
    out = jax.ShapeDtypeStruct((2, cells, ny, nz), F32)
    hbm = lambda x: pltpu.with_memory_space_constraint(x, pltpu.HBM)
    both = pl.pallas_call(
        functools.partial(kernel, n, spec),
        out_shape=out,
        in_specs=[pl.BlockSpec(memory_space=pltpu.HBM)] * 4,
        out_specs=vmem,
        scratch_shapes=[
            pltpu.SMEM((1,), F32), pltpu.VMEM(block_group.shape, jnp.int32),
            strip(8), fine(2), fine(4, 2), strip(8), fine(6), strip(8), strip(8), strip(8), strip(8),
            pltpu.VMEM((4, hy, nz), F32), fine(8), fine(8),
            coarse(n), coarse(n), coarse(n), coarse(n + 2), coarse(n + 2),
            pltpu.VMEM((TILES, n, hz), F32), pltpu.VMEM((TILES, n, hz), F32), pltpu.VMEM((TILES, n, hz), F32),
            dma(count), dma(count), dma(count), dma(count), dma(1), dma(1), dma(2, 2), dma(2, 2),
            dma(3, 3, 2), dma(3, 3, 2), dma(2), dma(2),
            dma(n // 2), dma(n // 2), dma(n), dma(3), dma(3),
            dma(2, n // 2), dma(2, n // 2), dma(2, n), dma(2), dma(2), dma(2), dma(2), dma(6), dma(6), dma(5),
        ],
        compiler_params=pltpu.CompilerParams(
            collective_id=0, has_side_effects=True, vmem_limit_bytes=(26 << 20) + 24 * n * hy * hz
        ),
    )(kappa, hbm(block_group), hbm(rhs.reshape(cells, ny, nz)), hbm(density))
    return both[:1], both[1:]


def solution(mesh):
    return jax.shard_map(
        functools.partial(local, mesh.shape["brick"], mesh.shape["spec"]),
        mesh=mesh,
        in_specs=(P("spec", "brick", None, None), P("brick", "spec", None), P("spec"), P()),
        out_specs=(P("spec", "brick", None, None), P("spec", "brick", None, None)),
        check_vma=False,
    )
```

```python
import functools

import jax
import jax.numpy as jnp
from jax import lax
from jax.experimental import pallas as pl
from jax.experimental.pallas import tpu as pltpu
from jax.sharding import PartitionSpec as P

TILES = 4
COARSE_SWEEPS = 3
relax_fine = 0.85
relax_coarse = 0.6
MESH = pl.DeviceIdType.MESH
F32 = jnp.float32
BF16 = jnp.bfloat16


def iota(shape, dim):
    return lax.broadcasted_iota(jnp.int32, shape, dim)


def split(x, parts):
    out = []
    for _ in range(parts):
        piece = x.astype(BF16)
        out.append(piece)
        x = x - piece.astype(F32)
    return out


def dot(a, b):
    return jnp.dot(a, b, preferred_element_type=F32)


def filter_rows(m):
    size = m.shape[0]
    row = iota(m.shape, 0)
    before = jnp.where(row == 0, 0.0, pltpu.roll(m, 1, 0))
    after = jnp.where(row == size - 1, 0.0, pltpu.roll(m, size - 1, 0))
    return m + 0.5 * (before + after)


def filter_lanes(m):
    size = m.shape[1]
    lane = iota(m.shape, 1)
    before = jnp.where(lane == 0, 0.0, pltpu.roll(m, 1, 1))
    after = jnp.where(lane == size - 1, 0.0, pltpu.roll(m, size - 1, 1))
    return m + 0.5 * (before + after)


def stencil(low, mid, high):
    return filter_lanes(filter_rows(mid + 0.5 * (low + high)))


def pair_matrix(fine, coarse):
    return (iota((coarse, fine), 1) // 2 == iota((coarse, fine), 0)).astype(BF16)


def pair_matrix_t(fine, coarse):
    return (iota((fine, coarse), 0) // 2 == iota((fine, coarse), 1)).astype(BF16)


def coarsen_sum(x, left=None):
    rows, cols = x.shape
    if left is None:
        left = pair_matrix(rows, rows // 2)
    right = pair_matrix_t(cols, cols // 2)
    halves = sum(dot(left, piece) for piece in split(x, 2))
    return sum(dot(piece, right) for piece in split(halves, 2)) * 0.125


def pieces_of(rows):
    units = rows // 8
    sizes = [max(1, round(units * share)) for share in (0.3, 0.3, 0.22, 0.12)]
    sizes.append(units - sum(sizes))
    starts = [sum(sizes[:c]) for c in range(len(sizes))]
    return [(8 * start, 8 * size) for start, size in zip(starts, sizes)]


def refine_layer(c):
    rows, cols = c.shape
    left = pair_matrix_t(2 * rows, rows)
    right = pair_matrix(2 * cols, cols)
    total = None
    for piece in split(c, 2):
        term = dot(dot(left, piece).astype(BF16), right)
        total = term if total is None else total + term
    return total


def kernel(
    n, spec, kappa_hbm, bg_hbm, rhs_ref, dens_ref, out_ref,
    kappa_ref, bg_ref,
    R, RF, D, IW, IE, V1, V2, W3, W4, WX, S, E3, CR, DC, CI, CA, CB, RS, DSUM, FX,
    prs, prr, frs, frr, rgs, rgr, dss, dsr, gss, gsr, dgs, dgr,
    azs, aps, ar, ass, asr, bzs, bps, br, w3s, w3r, w4s, w4r, xs, xr, ls,
):
    me = lax.axis_index("brick")
    j = lax.axis_index("spec")
    odd = lax.rem(me, 2)
    even = 1 - odd
    base = me - odd
    partner = base + even
    ny, nz = rhs_ref.shape[1], rhs_ref.shape[2]
    hy, hz = ny // 2, nz // 2
    rows = dens_ref.shape[1]
    half = n // 2
    window = R.shape[1]
    pieces = pieces_of(window)
    down, up = base > 0, base + 2 < n
    flow = jnp.logical_or(jnp.logical_and(odd == 0, down), jnp.logical_and(odd == 1, up))
    fhigh = jnp.logical_or(jnp.logical_and(odd == 0, up), jnp.logical_and(odd == 1, down))
    onward = lax.rem(me + 2 - 4 * odd + n, n)
    back = lax.rem(me - 2 + 4 * odd + n, n)
    below = lax.rem(me - 2 + n, n)
    above = lax.rem(me + 2, n)
    core = j + 1 - 2 * lax.rem(j, 2)
    far = lax.rem(j + spec // 2, spec)
    mine, theirs, near_slot, far_slot = 1 + odd, 2 - odd, 3 * odd, 3 - 3 * odd

    def remote(src, dst, ssem, rsem, b, s):
        return pltpu.make_async_remote_copy(
            src_ref=src, dst_ref=dst, send_sem=ssem, recv_sem=rsem,
            device_id={"brick": b, "spec": s}, device_id_type=MESH,
        )

    barrier = pltpu.get_barrier_semaphore()
    for k in range(1, half):
        pl.semaphore_signal(barrier, inc=1, device_id={"brick": lax.rem(me + 2 * k, n), "spec": j}, device_id_type=MESH)
    pl.semaphore_signal(barrier, inc=1, device_id={"brick": partner, "spec": j}, device_id_type=MESH)
    pl.semaphore_signal(barrier, inc=1, device_id={"brick": me, "spec": core}, device_id_type=MESH)
    pl.semaphore_signal(barrier, inc=1, device_id={"brick": me, "spec": far}, device_id_type=MESH)

    def eight(start, size):
        return pl.ds(pl.multiple_of(start, 8), size)

    far_core = lax.rem(core + spec // 2, spec)
    my_rows, core_rows, far_rows, far_core_rows = [eight(at * rows, rows) for at in (j, core, far, far_core)]
    crows = rows // 2
    cmine, ccore, cfar, cfarcore = [eight(at * crows, crows) for at in (j, core, far, far_core)]
    win = odd * (ny - window)
    their_win = even * (ny - window)
    lead = 8 * odd
    my_half, their_half = eight(odd * hy, hy), eight(even * hy, hy)
    loads = [
        pltpu.make_async_copy(dens_ref, D.at[mine, :, my_rows, :], ls.at[0]),
        pltpu.make_async_copy(kappa_hbm, kappa_ref, ls.at[1]),
        pltpu.make_async_copy(bg_hbm, bg_ref, ls.at[2]),
        pltpu.make_async_copy(rhs_ref.at[:, eight(win, window), :], R.at[pl.ds(2 * mine, 2)], ls.at[3]),
        pltpu.make_async_copy(rhs_ref, RF, ls.at[4]),
    ]
    for load in loads:
        load.start()

    blank = jnp.zeros((window, nz), F32)

    @pl.when(jnp.logical_not(down))
    def _():
        for buf, q in ((V1, 0), (V1, 1), (V2, 1), (W3, 1), (W4, 1)):
            buf[q] = blank

    @pl.when(jnp.logical_not(up))
    def _():
        for buf, q in ((V1, 6), (V1, 7), (V2, 6), (W3, 6), (W4, 6)):
            buf[q] = blank

    @pl.when(jnp.logical_not(flow))
    def _():
        WX[3 * odd] = jnp.zeros((hy, nz), F32)

    zero = jnp.zeros((hy, hz), F32)
    for buf in (CA, CB):
        buf[0] = zero
        buf[n + 1] = zero
    for load in loads[:3]:
        load.wait()
    kap = kappa_ref[0]
    kap1 = 0.25 * kap
    DC[me, cmine, :] = coarsen_sum(D[mine, 0, my_rows, :] + D[mine, 1, my_rows, :])
    pl.semaphore_wait(barrier, half - 1 + 3)

    def dpair(i, slot):
        return remote(dens_ref.at[i], D.at[slot, i, my_rows, :], dss.at[0, i], dsr.at[0, i], partner, j)

    def dfwd(i, dest):
        return remote(D.at[theirs, i, my_rows, :], D.at[near_slot, i, my_rows, :], dss.at[1, i], dsr.at[1, i], dest, j)

    def rpair(c, slot):
        start, size = pieces[c]
        return remote(
            rhs_ref.at[:, eight(their_win + start, size), :], R.at[pl.ds(2 * slot, 2), pl.ds(start, size), :],
            prs.at[c], prr.at[c], partner, j,
        )

    def rfwd(c, dest):
        start, size = pieces[c]
        return remote(
            R.at[pl.ds(2 * theirs, 2), pl.ds(start, size), :], R.at[pl.ds(2 * near_slot, 2), pl.ds(start, size), :],
            frs.at[c], frr.at[c], dest, j,
        )

    def rback(dest):
        return remote(rhs_ref.at[:, eight(win, window), :], R.at[pl.ds(2 * far_slot, 2)], rgs.at[0], rgr.at[0], dest, j)

    slots = (mine, theirs, near_slot)

    def dsrc(kind, i):
        return dens_ref.at[i] if kind == 0 else D.at[slots[kind], i, my_rows, :]

    def dfar(kind, i, at):
        return remote(dsrc(kind, i), D.at[slots[kind], i, at, :], gss.at[kind, 0, i], gsr.at[kind, 0, i], me, far)

    def dcore(kind, i, at):
        return remote(dsrc(kind, i), D.at[slots[kind], i, at, :], gss.at[kind, 1, i], gsr.at[kind, 1, i], me, core)

    def dcorefar(kind, i, at):
        return remote(
            D.at[slots[kind], i, far_rows, :], D.at[slots[kind], i, at, :], gss.at[kind, 2, i], gsr.at[kind, 2, i], me, core
        )

    strip = (hy + 16) // 2
    strip_win = odd * (hy - 16)

    def strip_rows(which):
        return eight(strip_win + strip * which, strip)

    lane_of = lax.rem(j, 2)

    def dback(dest):
        at = strip_rows(lane_of)
        return remote(D.at[mine, :, at, :], D.at[far_slot, :, at, :], dgs.at[0], dgr.at[0], dest, j)

    def dbackcore(which):
        at = strip_rows(which)
        return remote(D.at[far_slot, :, at, :], D.at[far_slot, :, at, :], dgs.at[1], dgr.at[1], me, core)

    def gather_start(view, zs, ps, rs):
        for k in range(1, half):
            remote(view(me), view(me), zs.at[k], rs.at[me], lax.rem(me + 2 * k, n), j).start()
        remote(view(me), view(me), ps.at[0], rs.at[me], partner, j).start()

    def gather_forward(view, zs, ps, rs):
        for k in range(1, half):
            b = lax.rem(me + 2 * k, n)
            remote(view(b), view(b), zs.at[k], rs.at[b], partner, j).wait_recv()
            remote(view(b), view(b), ps.at[k], rs.at[b], partner, j).start()

    def gather_finish(view, zs, ps, rs):
        for k in range(half):
            b = lax.rem(partner + 2 * k, n)
            remote(view(b), view(b), ps.at[k], rs.at[b], partner, j).wait_recv()

    def gather_sent(view, zs, ps, rs):
        for k in range(1, half):
            remote(view(me), view(me), zs.at[k], rs.at[me], partner, j).wait_send()
        for k in range(half):
            remote(view(me), view(me), ps.at[k], rs.at[me], partner, j).wait_send()

    dview = lambda b: DC.at[b, cmine, :]
    dgather = (dview, azs, aps, ar)
    for i in range(2):
        dpair(i, mine).start()
    for i in range(2):
        dfar(0, i, my_rows).start()
        dcore(0, i, my_rows).start()

    @pl.when(flow)
    def _():
        rback(back).start()

    gather_start(*dgather)
    dpair(0, mine).wait_send()
    rpair(0, mine).start()
    dpair(1, mine).wait_send()
    for c in range(1, len(pieces)):
        rpair(c, mine).start()

    def cfar_copy(at):
        return remote(DC.at[:, cmine, :], DC.at[:, at, :], ass.at[0], asr.at[0], me, far)

    def ccore_copy(at):
        return remote(DC.at[:, cmine, :], DC.at[:, at, :], ass.at[1], asr.at[1], me, core)

    def ccorefar_copy(at):
        return remote(DC.at[:, cfar, :], DC.at[:, at, :], ass.at[2], asr.at[2], me, core)

    def pass_on(c):
        rpair(c, theirs).wait_recv()

        @pl.when(fhigh)
        def _():
            rfwd(c, onward).start()

    def prepare(slot):
        def body(i, carry):
            inv = relax_fine / (D[slot, i, eight(win, window), :] + 14.0 * kap)
            IW[2 * slot + i] = inv
            V1[2 * slot + i] = R[2 * slot + i] * inv
            return carry

        lax.fori_loop(0, 2, body, 0)

    def layer(k):
        return k + odd * (7 - 2 * k)

    def relax_window(src, dst, q):
        v = src[q]
        f = stencil(src[q - 1], v, src[q + 1])
        dst[q] = (1.0 - relax_fine) * v + IW[q] * (R[q] + 2.0 * kap * (f - v))

    def residual_window(q):
        v = V2[q]
        f = stencil(V2[q - 1], v, V2[q + 1])
        d = D[q // 2, lax.rem(q, 2), eight(win, window), :]
        return R[q] - (d + 16.0 * kap) * v + 2.0 * kap * f

    chalf = hy // 2
    pick = (iota((chalf, window), 1) // 2 - lead // 2 == iota((chalf, window), 0)).astype(BF16)

    def coarse_rows_of(parity):
        return eight(parity * chalf, chalf)

    def rview(side, b):
        return CR.at[b if side else b + 1 - 2 * lax.rem(b, 2), coarse_rows_of(lax.rem(b, 2)), :]

    rgathers = [(functools.partial(rview, side), bzs.at[side], bps.at[side], br.at[side]) for side in range(2)]

    def restrict(q, brick):
        CR[brick, coarse_rows_of(odd), :] = coarsen_sum(residual_window(q) + residual_window(q + 1), pick)

    loads[3].wait()
    loads[4].wait()
    for i in range(2):
        dpair(i, theirs).wait_recv()

        @pl.when(fhigh)
        def _():
            dfwd(i, onward).start()

        dfar(1, i, my_rows).start()
        dcore(1, i, my_rows).start()
        dfar(0, i, far_rows).wait_recv()
        dcorefar(0, i, far_rows).start()

    for i in range(2):
        dcore(0, i, core_rows).wait_recv()
        dcorefar(0, i, far_core_rows).wait_recv()

    @pl.when(flow)
    def _():
        dback(back).start()

    prepare(mine)
    pass_on(0)

    @pl.when(flow)
    def _():
        for i in range(2):
            dfwd(i, back).wait_recv()
            dfar(2, i, my_rows).start()
            dcore(2, i, my_rows).start()

    pass_on(1)
    for i in range(2):
        dfar(1, i, far_rows).wait_recv()
        dcorefar(1, i, far_rows).start()
    pass_on(2)
    gather_forward(*dgather)
    for c in range(3, len(pieces)):
        pass_on(c)

    @pl.when(fhigh)
    def _():
        dback(onward).wait_recv()
        dbackcore(lane_of).start()

    for i in range(2):
        dcore(1, i, core_rows).wait_recv()
        dcorefar(1, i, far_core_rows).wait_recv()
    prepare(theirs)
    for k in (3, 4):
        relax_window(V1, V2, layer(k))

    @pl.when(flow)
    def _():
        for i in range(2):
            dfar(2, i, far_rows).wait_recv()
            dcorefar(2, i, far_rows).start()

    @pl.when(fhigh)
    def _():
        rback(onward).wait_recv()
        dbackcore(1 - lane_of).wait_recv()
        prepare(far_slot)

    relax_window(V1, V2, layer(5))

    @pl.when(fhigh)
    def _():
        relax_window(V1, V2, layer(6))

    restrict(4 - 2 * odd, base + even)
    gather_start(*rgathers[0])
    gather_finish(*dgather)
    cfar_copy(cmine).start()
    ccore_copy(cmine).start()

    @pl.when(flow)
    def _():
        for i in range(2):
            dcore(2, i, core_rows).wait_recv()
            dcorefar(2, i, far_core_rows).wait_recv()
        for c in range(len(pieces)):
            rfwd(c, back).wait_recv()
        prepare(near_slot)

    relax_window(V1, V2, layer(2))

    @pl.when(flow)
    def _():
        relax_window(V1, V2, layer(1))

    restrict(2 + 2 * odd, base + odd)

    gather_start(*rgathers[1])

    def edge_copy(buf, ss, rs, d, dest):
        return remote(buf.at[2 + 3 * d], buf.at[6 - 5 * d], ss.at[d], rs.at[d], dest, j)

    def edges_start(buf, ss, rs):
        @pl.when(down)
        def _():
            edge_copy(buf, ss, rs, 0, below).start()

        @pl.when(up)
        def _():
            edge_copy(buf, ss, rs, 1, above).start()

    def edges_finish(buf, ss, rs):
        @pl.when(up)
        def _():
            edge_copy(buf, ss, rs, 0, above).wait_recv()

        @pl.when(down)
        def _():
            edge_copy(buf, ss, rs, 1, below).wait_recv()

    def edges_sent(buf, ss, rs):
        @pl.when(down)
        def _():
            edge_copy(buf, ss, rs, 0, below).wait_send()

        @pl.when(up)
        def _():
            edge_copy(buf, ss, rs, 1, above).wait_send()

    part = hy // 2
    cross = [(3, 0, part), (3, part, part), (4, 0, part), (4, part, part), (5 - 3 * odd, 0, hy), (6 - 5 * odd, 0, hy)]
    cross_in = [(3, 0, part), (3, part, part), (4, 0, part), (4, part, part), (5 - 3 * even, 0, hy), (6 - 5 * even, 0, hy)]

    def wsend(c):
        q, start, size = cross[c]
        return remote(
            W4.at[q, eight(lead + start, size), :], WX.at[q - 3 + 2 * odd, pl.ds(start, size), :], xs.at[c], xr.at[c], partner, j
        )

    def wrecv(c):
        q, start, size = cross_in[c]
        return remote(
            W4.at[q, eight(lead + start, size), :], WX.at[q - 1 - 2 * odd, pl.ds(start, size), :], xs.at[c], xr.at[c], partner, j
        )

    relax_window(V2, W3, 2)
    relax_window(V2, W3, 5)

    def third_middle(q, carry):
        relax_window(V2, W3, q)
        return carry

    lax.fori_loop(3, 5, third_middle, 0)

    def fourth_middle(q, carry):
        relax_window(W3, W4, q)
        return carry

    lax.fori_loop(3, 5, fourth_middle, 0)
    for c in range(3):
        wsend(c).start()
    gather_forward(*rgathers[0])
    cfar_copy(cfar).wait_recv()
    ccorefar_copy(cfar).start()
    gather_forward(*rgathers[1])
    edges_start(W3, w3s, w3r)
    ccore_copy(ccore).wait_recv()
    ccorefar_copy(cfarcore).wait_recv()

    edge = hy // TILES
    lane_tile = iota((hz, hz), 0) // (hz // TILES) == iota((hz, hz), 1) // (hz // TILES)
    same_tile = lane_tile.astype(BF16)

    def lane_sums(x):
        return sum(dot(piece, same_tile) for piece in split(x, 3))

    bgf = bg_ref[...].astype(F32).astype(BF16)
    ids = []
    for ty in range(TILES):
        pick = iota((TILES * TILES, hz), 0) == ty * TILES + iota((TILES * TILES, hz), 1) // (hz // TILES)
        ids.append(dot(bgf, pick.astype(BF16)))

    brick_row = iota((n, hz), 0)
    lane = iota((n, hz), 1)
    tile_lanes = hz // TILES

    def lower_brick(x, fill):
        return jnp.where(brick_row == 0, fill, pltpu.roll(x, 1, 0))

    def upper_brick(x, fill):
        return jnp.where(brick_row == n - 1, fill, pltpu.roll(x, n - 1, 0))

    def group_sums(fields):
        out = []
        for ty in range(TILES):
            total = jnp.zeros((n, hz), F32)
            for b in range(n):
                total = total + jnp.where(ids[ty][b : b + 1] == ids[ty], fields[ty][b : b + 1], 0.0)
            out.append(total)
        return out

    def coarse_first(b, carry):
        d = DC[b]
        CI[b] = relax_fine / (d + 14.0 * kap1)
        for ty in range(TILES):
            DSUM[ty, pl.ds(b, 1), :] = jnp.sum(d[ty * edge : (ty + 1) * edge], axis=0, keepdims=True)
        return carry

    lax.fori_loop(0, n, coarse_first, 0)
    dens_sum = [lane_sums(DSUM[ty]) for ty in range(TILES)]
    weight = []
    for ty in range(TILES):
        fx = 1.0 + 0.5 * (lower_brick(ids[ty], -1.0) == ids[ty]).astype(F32)
        fx = fx + 0.5 * (upper_brick(ids[ty], -1.0) == ids[ty]).astype(F32)
        cells = edge * tile_lanes
        weight.append(16.0 * cells - 2.0 * (2 * edge - 1) * (2 * tile_lanes - 1) * fx)
    totals0 = group_sums(dens_sum)
    totals1 = group_sums(weight)
    step = [relax_coarse / (totals0[ty] + kap1 * totals1[ty]) for ty in range(TILES)]

    def invert(i, carry):
        IE[i] = relax_fine / (D[odd + i // 2, lax.rem(i, 2)] + 14.0 * kap)
        return carry

    lax.fori_loop(0, 6, invert, 0)
    edges_finish(W3, w3s, w3r)
    relax_window(W3, W4, 2)
    relax_window(W3, W4, 5)
    edges_start(W4, w4s, w4r)
    for rgather in rgathers:
        gather_finish(*rgather)
    wsend(3).start()
    wsend(4).start()

    def coarse_start(b, carry):
        CA[b + 1] = CR[b] * CI[b]
        return carry

    lax.fori_loop(0, n, coarse_start, 0)

    def coarse_defect(src, b):
        v = src[b + 1]
        f = stencil(src[b], v, src[b + 2])
        return v, CR[b] - (DC[b] + 16.0 * kap1) * v + 2.0 * kap1 * f

    def coarse_relax(src, dst):
        def body(b, carry):
            v = src[b + 1]
            f = stencil(src[b], v, src[b + 2])
            dst[b + 1] = (1.0 - relax_fine) * v + CI[b] * (CR[b] + 2.0 * kap1 * (f - v))
            return carry

        return body

    lax.fori_loop(0, n, coarse_relax(CA, CB), 0, unroll=2)

    def remainder(b, carry):
        defect = coarse_defect(CB, b)[1]
        for ty in range(TILES):
            RS[ty, pl.ds(b, 1), :] = jnp.sum(defect[ty * edge : (ty + 1) * edge], axis=0, keepdims=True)
        return carry

    lax.fori_loop(0, n, remainder, 0, unroll=2)
    group_rhs = group_sums([lane_sums(RS[ty]) for ty in range(TILES)])
    fix = [step[ty] * group_rhs[ty] for ty in range(TILES)]

    def aggregate_image(g):
        along = [x + 0.5 * (lower_brick(x, 0.0) + upper_brick(x, 0.0)) for x in g]
        blank = jnp.zeros((n, hz), F32)
        out = []
        for ty in range(TILES):
            below = along[ty - 1] if ty > 0 else blank
            above = along[ty + 1] if ty < TILES - 1 else blank
            mid = (2.0 * edge - 1.0) * along[ty] + 0.5 * (below + above)
            left = jnp.where(lane < tile_lanes, 0.0, pltpu.roll(mid, tile_lanes, 1))
            right = jnp.where(lane >= hz - tile_lanes, 0.0, pltpu.roll(mid, hz - tile_lanes, 1))
            f = (2.0 * tile_lanes - 1.0) * mid + 0.5 * (left + right)
            own = dens_sum[ty] + 16.0 * kap1 * (edge * tile_lanes)
            out.append(own * g[ty] - 2.0 * kap1 * f)
        return group_sums(out)

    for _ in range(COARSE_SWEEPS - 1):
        image = aggregate_image(fix)
        fix = [fix[ty] + step[ty] * (group_rhs[ty] - image[ty]) for ty in range(TILES)]
    for ty in range(TILES):
        FX[ty] = fix[ty]

    def add_fix(b, carry):
        for ty in range(TILES):
            part = pl.ds(ty * edge, edge)
            CA[b + 1, part, :] = CB[b + 1, part, :] + FX[ty, pl.ds(b, 1), :]
        return carry

    def near(width):
        return jnp.maximum(me - width, 0), jnp.minimum(me + width + 1, n)

    lax.fori_loop(*near(4), add_fix, 0)
    lax.fori_loop(*near(3), coarse_relax(CA, CB), 0)
    lax.fori_loop(*near(2), coarse_relax(CB, CA), 0)

    edges_finish(W4, w4s, w4r)

    @pl.when(fhigh)
    def _():
        wsend(5).start()

    def inside(e):
        g = 2 * me + e - 3
        return jnp.logical_and(g >= 0, g < 2 * n)

    for t in range(5):
        b = me + t - 2
        valid = jnp.logical_and(b >= 0, b < n)
        fine = jnp.where(valid, refine_layer(CA[jnp.clip(b, 0, n - 1) + 1]), 0.0)
        for e in (2 * t - 1, 2 * t):
            if 0 <= e < 8:
                S[e] = fine

    def relax_error(src, e):
        v = src[e]
        f = stencil(src[e - 1], v, src[e + 1])
        out = (1.0 - relax_fine) * v + IE[e - 1] * (2.0 * kap * (f - v))
        return jnp.where(inside(e), out, 0.0)

    def third(e, carry):
        E3[e] = relax_error(S, e)
        return carry

    lax.fori_loop(1, 7, third, 0, unroll=2)

    def fourth(e, carry):
        S[e] = relax_error(E3, e)
        q = e - 1 + 2 * odd
        S[e, my_half, :] = S[e, my_half, :] + W4[q, eight(lead, hy), :]
        return carry

    lax.fori_loop(2, 6, fourth, 0)
    for c in range(5):
        wrecv(c).wait_recv()

    @pl.when(flow)
    def _():
        wrecv(5).wait_recv()

    def join(e, carry):
        S[e, their_half, :] = S[e, their_half, :] + WX[e - 2]
        return carry

    lax.fori_loop(2, 6, join, 0)

    def last(i, carry):
        v = S[i + 3]
        out_ref[0, i] = v
        f = stencil(S[i + 2], v, S[i + 4])
        out_ref[1, i] = RF[i] - (D[mine, i] + 16.0 * kap) * v + 2.0 * kap * f
        return carry

    lax.fori_loop(0, 2, last, 0)

    for c in range(len(pieces)):
        rpair(c, mine).wait_send()
    for kind in (0, 1):
        for i in range(2):
            dfar(kind, i, my_rows).wait_send()
            dcore(kind, i, my_rows).wait_send()
            dcorefar(kind, i, far_rows).wait_send()

    @pl.when(flow)
    def _():
        rback(back).wait_send()
        dback(back).wait_send()
        for i in range(2):
            dfar(2, i, my_rows).wait_send()
            dcore(2, i, my_rows).wait_send()
            dcorefar(2, i, far_rows).wait_send()

    @pl.when(fhigh)
    def _():
        dbackcore(lane_of).wait_send()
        for i in range(2):
            dfwd(i, onward).wait_send()
        for c in range(len(pieces)):
            rfwd(c, onward).wait_send()

    gather_sent(*dgather)
    for rgather in rgathers:
        gather_sent(*rgather)
    cfar_copy(cmine).wait_send()
    ccore_copy(cmine).wait_send()
    ccorefar_copy(cfar).wait_send()
    edges_sent(W3, w3s, w3r)
    edges_sent(W4, w4s, w4r)
    for c in range(5):
        wsend(c).wait_send()

    @pl.when(fhigh)
    def _():
        wsend(5).wait_send()


def local(n, spec, rhs, density, kappa, block_group):
    _, cells, ny, nz = rhs.shape
    hy, hz = ny // 2, nz // 2
    window = hy + 8
    count = len(pieces_of(window))
    fine = lambda *lead: pltpu.VMEM(lead + (ny, nz), F32)
    strip = lambda *lead: pltpu.VMEM(lead + (window, nz), F32)
    coarse = lambda *lead: pltpu.VMEM(lead + (hy, hz), F32)
    dma = lambda *shape: pltpu.SemaphoreType.DMA(shape)
    vmem = pl.BlockSpec(memory_space=pltpu.VMEM)
    out = jax.ShapeDtypeStruct((2, cells, ny, nz), F32)
    hbm = lambda x: pltpu.with_memory_space_constraint(x, pltpu.HBM)
    both = pl.pallas_call(
        functools.partial(kernel, n, spec),
        out_shape=out,
        in_specs=[pl.BlockSpec(memory_space=pltpu.HBM)] * 4,
        out_specs=vmem,
        scratch_shapes=[
            pltpu.SMEM((1,), F32), pltpu.VMEM(block_group.shape, jnp.int32),
            strip(8), fine(2), fine(4, 2), strip(8), fine(6), strip(8), strip(8), strip(8), strip(8),
            pltpu.VMEM((4, hy, nz), F32), fine(8), fine(8),
            coarse(n), coarse(n), coarse(n), coarse(n + 2), coarse(n + 2),
            pltpu.VMEM((TILES, n, hz), F32), pltpu.VMEM((TILES, n, hz), F32), pltpu.VMEM((TILES, n, hz), F32),
            dma(count), dma(count), dma(count), dma(count), dma(1), dma(1), dma(2, 2), dma(2, 2),
            dma(3, 3, 2), dma(3, 3, 2), dma(2), dma(2),
            dma(n // 2), dma(n // 2), dma(n), dma(3), dma(3),
            dma(2, n // 2), dma(2, n // 2), dma(2, n), dma(2), dma(2), dma(2), dma(2), dma(6), dma(6), dma(5),
        ],
        compiler_params=pltpu.CompilerParams(
            collective_id=0, has_side_effects=True, vmem_limit_bytes=(26 << 20) + 24 * n * hy * hz
        ),
    )(kappa, hbm(block_group), hbm(rhs.reshape(cells, ny, nz)), hbm(density))
    return both[:1], both[1:]


def solution(mesh):
    return jax.shard_map(
        functools.partial(local, mesh.shape["brick"], mesh.shape["spec"]),
        mesh=mesh,
        in_specs=(P("spec", "brick", None, None), P("brick", "spec", None), P("spec"), P()),
        out_specs=(P("spec", "brick", None, None), P("spec", "brick", None, None)),
        check_vma=False,
    )
```

```python
import functools

import jax
import jax.numpy as jnp
from jax import lax
from jax.experimental import pallas as pl
from jax.experimental.pallas import tpu as pltpu
from jax.sharding import PartitionSpec as P

TILES = 4
COARSE_SWEEPS = 3
relax_fine = 0.85
relax_coarse = 0.6
MESH = pl.DeviceIdType.MESH
F32 = jnp.float32
BF16 = jnp.bfloat16


def iota(shape, dim):
    return lax.broadcasted_iota(jnp.int32, shape, dim)


def split(x, parts):
    out = []
    for _ in range(parts):
        piece = x.astype(BF16)
        out.append(piece)
        x = x - piece.astype(F32)
    return out


def dot(a, b):
    return jnp.dot(a, b, preferred_element_type=F32)


def filter_rows(m):
    size = m.shape[0]
    row = iota(m.shape, 0)
    before = jnp.where(row == 0, 0.0, pltpu.roll(m, 1, 0))
    after = jnp.where(row == size - 1, 0.0, pltpu.roll(m, size - 1, 0))
    return m + 0.5 * (before + after)


def filter_lanes(m):
    size = m.shape[1]
    lane = iota(m.shape, 1)
    before = jnp.where(lane == 0, 0.0, pltpu.roll(m, 1, 1))
    after = jnp.where(lane == size - 1, 0.0, pltpu.roll(m, size - 1, 1))
    return m + 0.5 * (before + after)


def stencil(low, mid, high):
    return filter_lanes(filter_rows(mid + 0.5 * (low + high)))


def pair_matrix(fine, coarse):
    return (iota((coarse, fine), 1) // 2 == iota((coarse, fine), 0)).astype(BF16)


def pair_matrix_t(fine, coarse):
    return (iota((fine, coarse), 0) // 2 == iota((fine, coarse), 1)).astype(BF16)


def coarsen_sum(x, left=None):
    rows, cols = x.shape
    if left is None:
        left = pair_matrix(rows, rows // 2)
    right = pair_matrix_t(cols, cols // 2)
    halves = sum(dot(left, piece) for piece in split(x, 2))
    return sum(dot(piece, right) for piece in split(halves, 2)) * 0.125


def pieces_of(rows):
    units = rows // 8
    sizes = [max(1, round(units * share)) for share in (0.3, 0.3, 0.22, 0.12)]
    sizes.append(units - sum(sizes))
    starts = [sum(sizes[:c]) for c in range(len(sizes))]
    return [(8 * start, 8 * size) for start, size in zip(starts, sizes)]


def refine_layer(c):
    rows, cols = c.shape
    left = pair_matrix_t(2 * rows, rows)
    right = pair_matrix(2 * cols, cols)
    total = None
    for piece in split(c, 2):
        term = dot(dot(left, piece).astype(BF16), right)
        total = term if total is None else total + term
    return total


def kernel(
    n, spec, kappa_hbm, bg_hbm, rhs_ref, dens_ref, out_ref,
    kappa_ref, bg_ref,
    R, RF, D, IW, IE, V1, V2, W3, W4, WX, S, E3, CR, DC, CI, CA, CB, RS, DSUM, FX,
    prs, prr, frs, frr, rgs, rgr, dss, dsr, gss, gsr, dgs, dgr,
    azs, aps, ar, ass, asr, bzs, bps, br, w3s, w3r, w4s, w4r, xs, xr, ls,
):
    me = lax.axis_index("brick")
    j = lax.axis_index("spec")
    odd = lax.rem(me, 2)
    even = 1 - odd
    base = me - odd
    partner = base + even
    ny, nz = rhs_ref.shape[1], rhs_ref.shape[2]
    hy, hz = ny // 2, nz // 2
    rows = dens_ref.shape[1]
    half = n // 2
    window = R.shape[1]
    pieces = pieces_of(window)
    down, up = base > 0, base + 2 < n
    flow = jnp.logical_or(jnp.logical_and(odd == 0, down), jnp.logical_and(odd == 1, up))
    fhigh = jnp.logical_or(jnp.logical_and(odd == 0, up), jnp.logical_and(odd == 1, down))
    onward = lax.rem(me + 2 - 4 * odd + n, n)
    back = lax.rem(me - 2 + 4 * odd + n, n)
    below = lax.rem(me - 2 + n, n)
    above = lax.rem(me + 2, n)
    core = j + 1 - 2 * lax.rem(j, 2)
    far = lax.rem(j + spec // 2, spec)
    mine, theirs, near_slot, far_slot = 1 + odd, 2 - odd, 3 * odd, 3 - 3 * odd

    def remote(src, dst, ssem, rsem, b, s):
        return pltpu.make_async_remote_copy(
            src_ref=src, dst_ref=dst, send_sem=ssem, recv_sem=rsem,
            device_id={"brick": b, "spec": s}, device_id_type=MESH,
        )

    barrier = pltpu.get_barrier_semaphore()
    for k in range(1, half):
        pl.semaphore_signal(barrier, inc=1, device_id={"brick": lax.rem(me + 2 * k, n), "spec": j}, device_id_type=MESH)
    pl.semaphore_signal(barrier, inc=1, device_id={"brick": partner, "spec": j}, device_id_type=MESH)
    pl.semaphore_signal(barrier, inc=1, device_id={"brick": me, "spec": core}, device_id_type=MESH)
    pl.semaphore_signal(barrier, inc=1, device_id={"brick": me, "spec": far}, device_id_type=MESH)

    def eight(start, size):
        return pl.ds(pl.multiple_of(start, 8), size)

    far_core = lax.rem(core + spec // 2, spec)
    my_rows, core_rows, far_rows, far_core_rows = [eight(at * rows, rows) for at in (j, core, far, far_core)]
    crows = rows // 2
    cmine, ccore, cfar, cfarcore = [eight(at * crows, crows) for at in (j, core, far, far_core)]
    win = odd * (ny - window)
    their_win = even * (ny - window)
    lead = 8 * odd
    my_half, their_half = eight(odd * hy, hy), eight(even * hy, hy)
    loads = [
        pltpu.make_async_copy(dens_ref, D.at[mine, :, my_rows, :], ls.at[0]),
        pltpu.make_async_copy(kappa_hbm, kappa_ref, ls.at[1]),
        pltpu.make_async_copy(bg_hbm, bg_ref, ls.at[2]),
        pltpu.make_async_copy(rhs_ref.at[:, eight(win, window), :], R.at[pl.ds(2 * mine, 2)], ls.at[3]),
        pltpu.make_async_copy(rhs_ref, RF, ls.at[4]),
    ]
    for load in loads:
        load.start()

    blank = jnp.zeros((window, nz), F32)

    @pl.when(jnp.logical_not(down))
    def _():
        for buf, q in ((V1, 0), (V1, 1), (V2, 1), (W3, 1), (W4, 1)):
            buf[q] = blank

    @pl.when(jnp.logical_not(up))
    def _():
        for buf, q in ((V1, 6), (V1, 7), (V2, 6), (W3, 6), (W4, 6)):
            buf[q] = blank

    @pl.when(jnp.logical_not(flow))
    def _():
        WX[3 * odd] = jnp.zeros((hy, nz), F32)

    zero = jnp.zeros((hy, hz), F32)
    for buf in (CA, CB):
        buf[0] = zero
        buf[n + 1] = zero
    for load in loads[:3]:
        load.wait()
    kap = kappa_ref[0]
    kap1 = 0.25 * kap
    DC[me, cmine, :] = coarsen_sum(D[mine, 0, my_rows, :] + D[mine, 1, my_rows, :])
    pl.semaphore_wait(barrier, half - 1 + 3)

    def dpair(i, slot):
        return remote(dens_ref.at[i], D.at[slot, i, my_rows, :], dss.at[0, i], dsr.at[0, i], partner, j)

    def dfwd(i, dest):
        return remote(D.at[theirs, i, my_rows, :], D.at[near_slot, i, my_rows, :], dss.at[1, i], dsr.at[1, i], dest, j)

    def rpair(c, slot):
        start, size = pieces[c]
        return remote(
            rhs_ref.at[:, eight(their_win + start, size), :], R.at[pl.ds(2 * slot, 2), pl.ds(start, size), :],
            prs.at[c], prr.at[c], partner, j,
        )

    def rfwd(c, dest):
        start, size = pieces[c]
        return remote(
            R.at[pl.ds(2 * theirs, 2), pl.ds(start, size), :], R.at[pl.ds(2 * near_slot, 2), pl.ds(start, size), :],
            frs.at[c], frr.at[c], dest, j,
        )

    def rback(dest):
        return remote(rhs_ref.at[:, eight(win, window), :], R.at[pl.ds(2 * far_slot, 2)], rgs.at[0], rgr.at[0], dest, j)

    slots = (mine, theirs, near_slot)

    def dsrc(kind, i):
        return dens_ref.at[i] if kind == 0 else D.at[slots[kind], i, my_rows, :]

    def dfar(kind, i, at):
        return remote(dsrc(kind, i), D.at[slots[kind], i, at, :], gss.at[kind, 0, i], gsr.at[kind, 0, i], me, far)

    def dcore(kind, i, at):
        return remote(dsrc(kind, i), D.at[slots[kind], i, at, :], gss.at[kind, 1, i], gsr.at[kind, 1, i], me, core)

    def dcorefar(kind, i, at):
        return remote(
            D.at[slots[kind], i, far_rows, :], D.at[slots[kind], i, at, :], gss.at[kind, 2, i], gsr.at[kind, 2, i], me, core
        )

    strip = (hy + 16) // 2
    strip_win = odd * (hy - 16)

    def strip_rows(which):
        return eight(strip_win + strip * which, strip)

    lane_of = lax.rem(j, 2)

    def dback(dest):
        at = strip_rows(lane_of)
        return remote(D.at[mine, :, at, :], D.at[far_slot, :, at, :], dgs.at[0], dgr.at[0], dest, j)

    def dbackcore(which):
        at = strip_rows(which)
        return remote(D.at[far_slot, :, at, :], D.at[far_slot, :, at, :], dgs.at[1], dgr.at[1], me, core)

    def gather_start(view, zs, ps, rs):
        for k in range(1, half):
            remote(view(me), view(me), zs.at[k], rs.at[me], lax.rem(me + 2 * k, n), j).start()
        remote(view(me), view(me), ps.at[0], rs.at[me], partner, j).start()

    def gather_forward(view, zs, ps, rs):
        for k in range(1, half):
            b = lax.rem(me + 2 * k, n)
            remote(view(b), view(b), zs.at[k], rs.at[b], partner, j).wait_recv()
            remote(view(b), view(b), ps.at[k], rs.at[b], partner, j).start()

    def gather_finish(view, zs, ps, rs):
        for k in range(half):
            b = lax.rem(partner + 2 * k, n)
            remote(view(b), view(b), ps.at[k], rs.at[b], partner, j).wait_recv()

    def gather_sent(view, zs, ps, rs):
        for k in range(1, half):
            remote(view(me), view(me), zs.at[k], rs.at[me], partner, j).wait_send()
        for k in range(half):
            remote(view(me), view(me), ps.at[k], rs.at[me], partner, j).wait_send()

    dview = lambda b: DC.at[b, cmine, :]
    dgather = (dview, azs, aps, ar)
    for i in range(2):
        dpair(i, mine).start()
    for i in range(2):
        dfar(0, i, my_rows).start()
        dcore(0, i, my_rows).start()

    @pl.when(flow)
    def _():
        rback(back).start()

    gather_start(*dgather)
    dpair(0, mine).wait_send()
    rpair(0, mine).start()
    dpair(1, mine).wait_send()
    for c in range(1, len(pieces)):
        rpair(c, mine).start()

    def cfar_copy(at):
        return remote(DC.at[:, cmine, :], DC.at[:, at, :], ass.at[0], asr.at[0], me, far)

    def ccore_copy(at):
        return remote(DC.at[:, cmine, :], DC.at[:, at, :], ass.at[1], asr.at[1], me, core)

    def ccorefar_copy(at):
        return remote(DC.at[:, cfar, :], DC.at[:, at, :], ass.at[2], asr.at[2], me, core)

    def pass_on(c):
        rpair(c, theirs).wait_recv()

        @pl.when(fhigh)
        def _():
            rfwd(c, onward).start()

    def prepare(slot):
        def body(i, carry):
            inv = relax_fine / (D[slot, i, eight(win, window), :] + 14.0 * kap)
            IW[2 * slot + i] = inv
            V1[2 * slot + i] = R[2 * slot + i] * inv
            return carry

        lax.fori_loop(0, 2, body, 0)

    def layer(k):
        return k + odd * (7 - 2 * k)

    def relax_window(src, dst, q):
        v = src[q]
        f = stencil(src[q - 1], v, src[q + 1])
        dst[q] = (1.0 - relax_fine) * v + IW[q] * (R[q] + 2.0 * kap * (f - v))

    def residual_window(q):
        v = V2[q]
        f = stencil(V2[q - 1], v, V2[q + 1])
        d = D[q // 2, lax.rem(q, 2), eight(win, window), :]
        return R[q] - (d + 16.0 * kap) * v + 2.0 * kap * f

    chalf = hy // 2
    pick = (iota((chalf, window), 1) // 2 - lead // 2 == iota((chalf, window), 0)).astype(BF16)

    def coarse_rows_of(parity):
        return eight(parity * chalf, chalf)

    def rview(side, b):
        return CR.at[b if side else b + 1 - 2 * lax.rem(b, 2), coarse_rows_of(lax.rem(b, 2)), :]

    rgathers = [(functools.partial(rview, side), bzs.at[side], bps.at[side], br.at[side]) for side in range(2)]

    def restrict(q, brick):
        CR[brick, coarse_rows_of(odd), :] = coarsen_sum(residual_window(q) + residual_window(q + 1), pick)

    loads[3].wait()
    loads[4].wait()
    for i in range(2):
        dpair(i, theirs).wait_recv()

        @pl.when(fhigh)
        def _():
            dfwd(i, onward).start()

        dfar(1, i, my_rows).start()
        dcore(1, i, my_rows).start()
        dfar(0, i, far_rows).wait_recv()
        dcorefar(0, i, far_rows).start()

    for i in range(2):
        dcore(0, i, core_rows).wait_recv()
        dcorefar(0, i, far_core_rows).wait_recv()

    @pl.when(flow)
    def _():
        dback(back).start()

    prepare(mine)
    pass_on(0)

    @pl.when(flow)
    def _():
        for i in range(2):
            dfwd(i, back).wait_recv()
            dfar(2, i, my_rows).start()
            dcore(2, i, my_rows).start()

    pass_on(1)
    for i in range(2):
        dfar(1, i, far_rows).wait_recv()
        dcorefar(1, i, far_rows).start()
    pass_on(2)
    gather_forward(*dgather)
    for c in range(3, len(pieces)):
        pass_on(c)

    @pl.when(fhigh)
    def _():
        dback(onward).wait_recv()
        dbackcore(lane_of).start()

    for i in range(2):
        dcore(1, i, core_rows).wait_recv()
        dcorefar(1, i, far_core_rows).wait_recv()
    prepare(theirs)
    for k in (3, 4):
        relax_window(V1, V2, layer(k))

    @pl.when(flow)
    def _():
        for i in range(2):
            dfar(2, i, far_rows).wait_recv()
            dcorefar(2, i, far_rows).start()

    @pl.when(fhigh)
    def _():
        rback(onward).wait_recv()
        dbackcore(1 - lane_of).wait_recv()
        prepare(far_slot)

    relax_window(V1, V2, layer(5))

    @pl.when(fhigh)
    def _():
        relax_window(V1, V2, layer(6))

    restrict(4 - 2 * odd, base + even)
    gather_start(*rgathers[0])
    gather_finish(*dgather)
    cfar_copy(cmine).start()
    ccore_copy(cmine).start()

    @pl.when(flow)
    def _():
        for i in range(2):
            dcore(2, i, core_rows).wait_recv()
            dcorefar(2, i, far_core_rows).wait_recv()
        for c in range(len(pieces)):
            rfwd(c, back).wait_recv()
        prepare(near_slot)

    relax_window(V1, V2, layer(2))

    @pl.when(flow)
    def _():
        relax_window(V1, V2, layer(1))

    restrict(2 + 2 * odd, base + odd)

    gather_start(*rgathers[1])

    def edge_copy(buf, ss, rs, d, dest):
        return remote(buf.at[2 + 3 * d], buf.at[6 - 5 * d], ss.at[d], rs.at[d], dest, j)

    def edges_start(buf, ss, rs):
        @pl.when(down)
        def _():
            edge_copy(buf, ss, rs, 0, below).start()

        @pl.when(up)
        def _():
            edge_copy(buf, ss, rs, 1, above).start()

    def edges_finish(buf, ss, rs):
        @pl.when(up)
        def _():
            edge_copy(buf, ss, rs, 0, above).wait_recv()

        @pl.when(down)
        def _():
            edge_copy(buf, ss, rs, 1, below).wait_recv()

    def edges_sent(buf, ss, rs):
        @pl.when(down)
        def _():
            edge_copy(buf, ss, rs, 0, below).wait_send()

        @pl.when(up)
        def _():
            edge_copy(buf, ss, rs, 1, above).wait_send()

    part = hy // 2
    cross = [(3, 0, part), (3, part, part), (4, 0, part), (4, part, part), (5 - 3 * odd, 0, hy), (6 - 5 * odd, 0, hy)]
    cross_in = [(3, 0, part), (3, part, part), (4, 0, part), (4, part, part), (5 - 3 * even, 0, hy), (6 - 5 * even, 0, hy)]

    def wsend(c):
        q, start, size = cross[c]
        return remote(
            W4.at[q, eight(lead + start, size), :], WX.at[q - 3 + 2 * odd, pl.ds(start, size), :], xs.at[c], xr.at[c], partner, j
        )

    def wrecv(c):
        q, start, size = cross_in[c]
        return remote(
            W4.at[q, eight(lead + start, size), :], WX.at[q - 1 - 2 * odd, pl.ds(start, size), :], xs.at[c], xr.at[c], partner, j
        )

    relax_window(V2, W3, 2)
    relax_window(V2, W3, 5)

    def third_middle(q, carry):
        relax_window(V2, W3, q)
        return carry

    lax.fori_loop(3, 5, third_middle, 0)

    def fourth_middle(q, carry):
        relax_window(W3, W4, q)
        return carry

    lax.fori_loop(3, 5, fourth_middle, 0)
    for c in range(3):
        wsend(c).start()
    gather_forward(*rgathers[0])
    edges_start(W3, w3s, w3r)
    cfar_copy(cfar).wait_recv()
    ccorefar_copy(cfar).start()
    gather_forward(*rgathers[1])
    ccore_copy(ccore).wait_recv()
    ccorefar_copy(cfarcore).wait_recv()

    edge = hy // TILES
    lane_tile = iota((hz, hz), 0) // (hz // TILES) == iota((hz, hz), 1) // (hz // TILES)
    same_tile = lane_tile.astype(BF16)

    def lane_sums(x):
        return sum(dot(piece, same_tile) for piece in split(x, 3))

    bgf = bg_ref[...].astype(F32).astype(BF16)
    ids = []
    for ty in range(TILES):
        pick = iota((TILES * TILES, hz), 0) == ty * TILES + iota((TILES * TILES, hz), 1) // (hz // TILES)
        ids.append(dot(bgf, pick.astype(BF16)))

    brick_row = iota((n, hz), 0)
    lane = iota((n, hz), 1)
    tile_lanes = hz // TILES

    def lower_brick(x, fill):
        return jnp.where(brick_row == 0, fill, pltpu.roll(x, 1, 0))

    def upper_brick(x, fill):
        return jnp.where(brick_row == n - 1, fill, pltpu.roll(x, n - 1, 0))

    def group_sums(fields):
        out = []
        for ty in range(TILES):
            total = jnp.zeros((n, hz), F32)
            for b in range(n):
                total = total + jnp.where(ids[ty][b : b + 1] == ids[ty], fields[ty][b : b + 1], 0.0)
            out.append(total)
        return out

    def coarse_first(b, carry):
        d = DC[b]
        CI[b] = relax_fine / (d + 14.0 * kap1)
        for ty in range(TILES):
            DSUM[ty, pl.ds(b, 1), :] = jnp.sum(d[ty * edge : (ty + 1) * edge], axis=0, keepdims=True)
        return carry

    lax.fori_loop(0, n, coarse_first, 0)
    dens_sum = [lane_sums(DSUM[ty]) for ty in range(TILES)]
    weight = []
    for ty in range(TILES):
        fx = 1.0 + 0.5 * (lower_brick(ids[ty], -1.0) == ids[ty]).astype(F32)
        fx = fx + 0.5 * (upper_brick(ids[ty], -1.0) == ids[ty]).astype(F32)
        cells = edge * tile_lanes
        weight.append(16.0 * cells - 2.0 * (2 * edge - 1) * (2 * tile_lanes - 1) * fx)
    totals0 = group_sums(dens_sum)
    totals1 = group_sums(weight)
    step = [relax_coarse / (totals0[ty] + kap1 * totals1[ty]) for ty in range(TILES)]

    def invert(i, carry):
        IE[i] = relax_fine / (D[odd + i // 2, lax.rem(i, 2)] + 14.0 * kap)
        return carry

    lax.fori_loop(0, 6, invert, 0)
    edges_finish(W3, w3s, w3r)
    relax_window(W3, W4, 2)
    relax_window(W3, W4, 5)
    edges_start(W4, w4s, w4r)
    for rgather in rgathers:
        gather_finish(*rgather)
    wsend(3).start()
    wsend(4).start()

    def coarse_start(b, carry):
        CA[b + 1] = CR[b] * CI[b]
        return carry

    lax.fori_loop(0, n, coarse_start, 0)

    def coarse_defect(src, b):
        v = src[b + 1]
        f = stencil(src[b], v, src[b + 2])
        return v, CR[b] - (DC[b] + 16.0 * kap1) * v + 2.0 * kap1 * f

    def coarse_relax(src, dst):
        def body(b, carry):
            v = src[b + 1]
            f = stencil(src[b], v, src[b + 2])
            dst[b + 1] = (1.0 - relax_fine) * v + CI[b] * (CR[b] + 2.0 * kap1 * (f - v))
            return carry

        return body

    lax.fori_loop(0, n, coarse_relax(CA, CB), 0, unroll=2)

    def remainder(b, carry):
        defect = coarse_defect(CB, b)[1]
        for ty in range(TILES):
            RS[ty, pl.ds(b, 1), :] = jnp.sum(defect[ty * edge : (ty + 1) * edge], axis=0, keepdims=True)
        return carry

    lax.fori_loop(0, n, remainder, 0, unroll=2)
    group_rhs = group_sums([lane_sums(RS[ty]) for ty in range(TILES)])
    fix = [step[ty] * group_rhs[ty] for ty in range(TILES)]

    def aggregate_image(g):
        along = [x + 0.5 * (lower_brick(x, 0.0) + upper_brick(x, 0.0)) for x in g]
        blank = jnp.zeros((n, hz), F32)
        out = []
        for ty in range(TILES):
            below = along[ty - 1] if ty > 0 else blank
            above = along[ty + 1] if ty < TILES - 1 else blank
            mid = (2.0 * edge - 1.0) * along[ty] + 0.5 * (below + above)
            left = jnp.where(lane < tile_lanes, 0.0, pltpu.roll(mid, tile_lanes, 1))
            right = jnp.where(lane >= hz - tile_lanes, 0.0, pltpu.roll(mid, hz - tile_lanes, 1))
            f = (2.0 * tile_lanes - 1.0) * mid + 0.5 * (left + right)
            own = dens_sum[ty] + 16.0 * kap1 * (edge * tile_lanes)
            out.append(own * g[ty] - 2.0 * kap1 * f)
        return group_sums(out)

    for _ in range(COARSE_SWEEPS - 1):
        image = aggregate_image(fix)
        fix = [fix[ty] + step[ty] * (group_rhs[ty] - image[ty]) for ty in range(TILES)]
    for ty in range(TILES):
        FX[ty] = fix[ty]

    def add_fix(b, carry):
        for ty in range(TILES):
            part = pl.ds(ty * edge, edge)
            CA[b + 1, part, :] = CB[b + 1, part, :] + FX[ty, pl.ds(b, 1), :]
        return carry

    def near(width):
        return jnp.maximum(me - width, 0), jnp.minimum(me + width + 1, n)

    lax.fori_loop(*near(4), add_fix, 0)
    lax.fori_loop(*near(3), coarse_relax(CA, CB), 0)
    lax.fori_loop(*near(2), coarse_relax(CB, CA), 0)

    edges_finish(W4, w4s, w4r)

    @pl.when(fhigh)
    def _():
        wsend(5).start()

    def inside(e):
        g = 2 * me + e - 3
        return jnp.logical_and(g >= 0, g < 2 * n)

    for t in range(5):
        b = me + t - 2
        valid = jnp.logical_and(b >= 0, b < n)
        fine = jnp.where(valid, refine_layer(CA[jnp.clip(b, 0, n - 1) + 1]), 0.0)
        for e in (2 * t - 1, 2 * t):
            if 0 <= e < 8:
                S[e] = fine

    def relax_error(src, e):
        v = src[e]
        f = stencil(src[e - 1], v, src[e + 1])
        out = (1.0 - relax_fine) * v + IE[e - 1] * (2.0 * kap * (f - v))
        return jnp.where(inside(e), out, 0.0)

    def third(e, carry):
        E3[e] = relax_error(S, e)
        return carry

    lax.fori_loop(1, 7, third, 0, unroll=2)

    def fourth(e, carry):
        S[e] = relax_error(E3, e)
        q = e - 1 + 2 * odd
        S[e, my_half, :] = S[e, my_half, :] + W4[q, eight(lead, hy), :]
        return carry

    lax.fori_loop(2, 6, fourth, 0)
    for c in range(5):
        wrecv(c).wait_recv()

    @pl.when(flow)
    def _():
        wrecv(5).wait_recv()

    def join(e, carry):
        S[e, their_half, :] = S[e, their_half, :] + WX[e - 2]
        return carry

    lax.fori_loop(2, 6, join, 0)

    def last(i, carry):
        v = S[i + 3]
        out_ref[0, i] = v
        f = stencil(S[i + 2], v, S[i + 4])
        out_ref[1, i] = RF[i] - (D[mine, i] + 16.0 * kap) * v + 2.0 * kap * f
        return carry

    lax.fori_loop(0, 2, last, 0)

    for c in range(len(pieces)):
        rpair(c, mine).wait_send()
    for kind in (0, 1):
        for i in range(2):
            dfar(kind, i, my_rows).wait_send()
            dcore(kind, i, my_rows).wait_send()
            dcorefar(kind, i, far_rows).wait_send()

    @pl.when(flow)
    def _():
        rback(back).wait_send()
        dback(back).wait_send()
        for i in range(2):
            dfar(2, i, my_rows).wait_send()
            dcore(2, i, my_rows).wait_send()
            dcorefar(2, i, far_rows).wait_send()

    @pl.when(fhigh)
    def _():
        dbackcore(lane_of).wait_send()
        for i in range(2):
            dfwd(i, onward).wait_send()
        for c in range(len(pieces)):
            rfwd(c, onward).wait_send()

    gather_sent(*dgather)
    for rgather in rgathers:
        gather_sent(*rgather)
    cfar_copy(cmine).wait_send()
    ccore_copy(cmine).wait_send()
    ccorefar_copy(cfar).wait_send()
    edges_sent(W3, w3s, w3r)
    edges_sent(W4, w4s, w4r)
    for c in range(5):
        wsend(c).wait_send()

    @pl.when(fhigh)
    def _():
        wsend(5).wait_send()


def local(n, spec, rhs, density, kappa, block_group):
    _, cells, ny, nz = rhs.shape
    hy, hz = ny // 2, nz // 2
    window = hy + 8
    count = len(pieces_of(window))
    fine = lambda *lead: pltpu.VMEM(lead + (ny, nz), F32)
    strip = lambda *lead: pltpu.VMEM(lead + (window, nz), F32)
    coarse = lambda *lead: pltpu.VMEM(lead + (hy, hz), F32)
    dma = lambda *shape: pltpu.SemaphoreType.DMA(shape)
    vmem = pl.BlockSpec(memory_space=pltpu.VMEM)
    out = jax.ShapeDtypeStruct((2, cells, ny, nz), F32)
    hbm = lambda x: pltpu.with_memory_space_constraint(x, pltpu.HBM)
    both = pl.pallas_call(
        functools.partial(kernel, n, spec),
        out_shape=out,
        in_specs=[pl.BlockSpec(memory_space=pltpu.HBM)] * 4,
        out_specs=vmem,
        scratch_shapes=[
            pltpu.SMEM((1,), F32), pltpu.VMEM(block_group.shape, jnp.int32),
            strip(8), fine(2), fine(4, 2), strip(8), fine(6), strip(8), strip(8), strip(8), strip(8),
            pltpu.VMEM((4, hy, nz), F32), fine(8), fine(8),
            coarse(n), coarse(n), coarse(n), coarse(n + 2), coarse(n + 2),
            pltpu.VMEM((TILES, n, hz), F32), pltpu.VMEM((TILES, n, hz), F32), pltpu.VMEM((TILES, n, hz), F32),
            dma(count), dma(count), dma(count), dma(count), dma(1), dma(1), dma(2, 2), dma(2, 2),
            dma(3, 3, 2), dma(3, 3, 2), dma(2), dma(2),
            dma(n // 2), dma(n // 2), dma(n), dma(3), dma(3),
            dma(2, n // 2), dma(2, n // 2), dma(2, n), dma(2), dma(2), dma(2), dma(2), dma(6), dma(6), dma(5),
        ],
        compiler_params=pltpu.CompilerParams(
            collective_id=0, has_side_effects=True, vmem_limit_bytes=(26 << 20) + 24 * n * hy * hz
        ),
    )(kappa, hbm(block_group), hbm(rhs.reshape(cells, ny, nz)), hbm(density))
    return both[:1], both[1:]


def solution(mesh):
    return jax.shard_map(
        functools.partial(local, mesh.shape["brick"], mesh.shape["spec"]),
        mesh=mesh,
        in_specs=(P("spec", "brick", None, None), P("brick", "spec", None), P("spec"), P()),
        out_specs=(P("spec", "brick", None, None), P("spec", "brick", None, None)),
        check_vma=False,
    )
```
